256 devices in a mesh: adapter: 64 (over x, z, core), tensor: 4 (over y).
Axes of the slice: x: 4, y: 4, z: 8, core: 2. Of those that a mesh axis runs over, the one named last changes fastest.
Arguments:
- activations: bfloat16 [32768, 4096], P('adapter', 'tensor'), may hold values from -6 to 6
- output_gradient: bfloat16 [32768, 4096], P('adapter', 'tensor'), may hold values from -6 to 6
- frozen_weight: bfloat16 [4096, 4096], P(None, 'tensor'), may hold values from -0.09375 to 0.09375
- adapter_down_weight: bfloat16 [8192, 4096], P('adapter', 'tensor'), may hold values from -0.09375 to 0.09375
- adapter_up_weight: bfloat16 [8192, 4096], P('adapter', 'tensor'), may hold values from -0.09375 to 0.09375
- adapter_slot_table: int32 [512], replicated, may hold values from 0 to 511, as said below
- group_adapter_index: int32 [64, 48], P('adapter'), may hold values from 0 to 511, as said below
- group_token_length: int32 [64, 48], P('adapter'), may hold values from 1 to 16, as said below
Outputs:
- input_gradient: bfloat16 [32768, 4096], P('adapter', 'tensor')
- down_grad: float32 [8192, 4096], P('adapter', 'tensor')
- up_grad: float32 [8192, 4096], P('adapter', 'tensor')
The draws below stay inside these ranges and needn't reach their ends.
Inputs may be any that keep to these rules, and one draw needn't show every extreme that they name: `adapter_slot_table`: a permutation of the slots; slot k lies on adapter index k // 8. `group_adapter_index`: the adapters of one index's groups lie on distinct indices of the adapter axis; on every index one group of exactly 16 tokens uses an adapter stored on one index that is the same for all indices. `group_token_length`: each row sums to 512 and holds a group of exactly 16 tokens.
All inputs are finite; a program needn't handle non-finite values.
Results may differ from the reference program's by a relative error of at most 0.015.
Values may be sent and summed in bfloat16 or wider, within the bound.
A program may use at most 128 MiB of HBM per device.

```python
import jax
import jax.numpy as jnp
from jax import lax

INPUT_FEATURES = 4096
OUTPUT_FEATURES = 4096
ADAPTER_RANK = 16
ADP_DEV = 8
TOK_DEV = 512
ADAPTER_TOTAL = 512
TOKENS = 32768
NGROUPS = 48
PEER_ROWS = 16
N_ADAPTER = 64
N_TENSOR = 4


def shared_layout(key):
    slot_perm = jax.random.permutation(jax.random.fold_in(key, 11), ADAPTER_TOTAL).astype(jnp.int32)
    hot_owner = jax.random.randint(jax.random.fold_in(key, 12), (), 0, N_ADAPTER).astype(jnp.int32)
    start_at = jax.random.randint(jax.random.fold_in(key, 13), (N_ADAPTER,), 0, NGROUPS).astype(jnp.int32)
    return (slot_perm, hot_owner, start_at)


def draw_adapter_slot_table(key, part):
    return shared_layout(key)[0]


def owner_row(row_key, hot_owner, start_at):
    others = jax.random.permutation(row_key, N_ADAPTER - 1).astype(jnp.int32)
    owners = jnp.concatenate([hot_owner[None], (hot_owner + 1 + others[:NGROUPS - 1]) % N_ADAPTER])
    return jnp.roll(owners, start_at)


def draw_group_adapter_index(key, part):
    slot_perm, hot_owner, start_at = shared_layout(key)
    inverse = jnp.argsort(slot_perm, stable=True).astype(jnp.int32)
    row_keys = jax.random.split(jax.random.fold_in(key, 14), N_ADAPTER)
    owners = jax.vmap(owner_row, in_axes=(0, None, 0))(row_keys, hot_owner, start_at)
    local_slot = jax.random.randint(jax.random.fold_in(key, 15), (N_ADAPTER, NGROUPS), 0, ADP_DEV).astype(jnp.int32)
    return inverse[owners * ADP_DEV + local_slot].astype(jnp.int32)


def draw_group_token_length(key, part):
    start_at = shared_layout(key)[2]
    remain = TOK_DEV - PEER_ROWS
    others = NGROUPS - 1
    common = remain // others
    spare = remain % others
    lowest = max(1 - common, common + 2 - PEER_ROWS)
    highest = min(common - 1, PEER_ROWS - common - 2)
    if lowest > 0 or highest < 0:
        lowest = 0
        highest = 0
    lengths = common + (jnp.arange(others) < spare).astype(jnp.int32)
    pairs = others // 2
    change = jax.random.randint(jax.random.fold_in(key, 16), (N_ADAPTER, pairs), lowest, highest + 1).astype(jnp.int32)
    signed = jnp.stack([change, -change], axis=2).reshape(N_ADAPTER, 2 * pairs)
    if others % 2 == 1:
        signed = jnp.concatenate([signed, jnp.zeros((N_ADAPTER, 1), jnp.int32)], axis=1)
    rest_rows = lengths[None, :] + signed
    full_rows = jnp.concatenate([jnp.full((N_ADAPTER, 1), PEER_ROWS, jnp.int32), rest_rows], axis=1)
    return jax.vmap(jnp.roll)(full_rows, start_at).astype(jnp.int32)


def block_levels(key, dims, cuts, low, top_value):
    gain, own = 1.0, jax.random.fold_in(key, 6)
    for axis_at, blocks in cuts:
        draws = jnp.exp(jax.random.uniform(jax.random.fold_in(own, axis_at), (blocks,), jnp.float32, low / len(cuts), top_value / len(cuts)))
        gain = gain * jnp.repeat(draws, dims[axis_at] // blocks).reshape([-1 if axis == axis_at else 1 for axis in range(len(dims))])
    return gain


def normal_values(own_key, shape, width, reach, shards=(), kind=jnp.bfloat16):
    gain = block_levels(own_key, shape, shards, -0.22, 0.18) if shards else 1.0
    drawn = jax.random.normal(own_key, shape, jnp.float32) * width * gain
    return jnp.minimum(jnp.maximum(drawn, -reach), reach).astype(kind)


def setup_inputs(seed: int = 0) -> dict:
    seeds = jax.random.split(jax.random.key(seed), 9)
    activations = normal_values(seeds[0], (TOKENS, INPUT_FEATURES), 1.0, 6.0, ((0, 64), (1, 4)))
    output_gradient = normal_values(seeds[1], (TOKENS, OUTPUT_FEATURES), 1.0, 6.0, ((0, 64), (1, 4)))
    frozen_weight = normal_values(seeds[2], (INPUT_FEATURES, OUTPUT_FEATURES), OUTPUT_FEATURES ** -0.5, 0.09375, ((1, 4),))
    adapter_down_weight = normal_values(seeds[3], (ADAPTER_TOTAL * ADAPTER_RANK, INPUT_FEATURES), INPUT_FEATURES ** -0.5, 0.09375, ((0, 64), (1, 4)))
    adapter_up_weight = normal_values(seeds[4], (ADAPTER_TOTAL * ADAPTER_RANK, OUTPUT_FEATURES), OUTPUT_FEATURES ** -0.5, 0.09375, ((0, 64), (1, 4)))
    adapter_slot_table = draw_adapter_slot_table(jax.random.fold_in(seeds[8], 71), 0)
    group_adapter_index = draw_group_adapter_index(jax.random.fold_in(seeds[8], 71), 0)
    group_token_length = draw_group_token_length(jax.random.fold_in(seeds[8], 71), 0)
    return dict(activations=activations, output_gradient=output_gradient, frozen_weight=frozen_weight, adapter_down_weight=adapter_down_weight, adapter_up_weight=adapter_up_weight, adapter_slot_table=adapter_slot_table, group_adapter_index=group_adapter_index, group_token_length=group_token_length)


adapter_scale = 2.0


def reference(activations, output_gradient, frozen_weight, adapter_down_weight, adapter_up_weight, adapter_slot_table, group_adapter_index, group_token_length):
    down_matrices = adapter_down_weight.reshape(ADAPTER_TOTAL, ADAPTER_RANK, INPUT_FEATURES)
    up_matrices = adapter_up_weight.reshape(ADAPTER_TOTAL, ADAPTER_RANK, OUTPUT_FEATURES)
    positions = jnp.arange(TOK_DEV, dtype=jnp.int32)
    block = OUTPUT_FEATURES // N_TENSOR

    def device_step(carry, device):
        grad_down, grad_up = carry
        input_rows_local = lax.dynamic_slice_in_dim(activations, device * TOK_DEV, TOK_DEV, 0)
        gradient_rows = lax.dynamic_slice_in_dim(output_gradient, device * TOK_DEV, TOK_DEV, 0)
        lengths = group_token_length[device]
        group_ends = jnp.cumsum(lengths).astype(jnp.int32)
        tok_group = jnp.sum((positions[:, None] >= group_ends[None, :]).astype(jnp.int32), axis=1)
        group_slots = adapter_slot_table[group_adapter_index[device]].astype(jnp.int32)
        tok_slot = group_slots[tok_group].astype(jnp.int32)
        down_block_rows = down_matrices[tok_slot].astype(jnp.float32)
        up_rows = up_matrices[tok_slot].astype(jnp.float32)
        down_proj = jnp.einsum("td,trd->tr", input_rows_local.astype(jnp.float32), down_block_rows)
        up_proj = jnp.einsum("td,trd->tr", gradient_rows.astype(jnp.float32), up_rows)
        down_reduced = down_proj.astype(jnp.bfloat16)
        up_reduced = up_proj.astype(jnp.bfloat16)
        adapter_input_grad = (adapter_scale * jnp.einsum("sp,spa->sa", up_reduced.astype(jnp.float32), down_block_rows)).astype(jnp.bfloat16)
        frozen_input_grad = jnp.zeros((TOK_DEV, INPUT_FEATURES), jnp.float32)
        for part in range(N_TENSOR):
            piece = jnp.dot(gradient_rows[:, part * block:(part + 1) * block], frozen_weight[:, part * block:(part + 1) * block].T, preferred_element_type=jnp.float32)
            frozen_input_grad = frozen_input_grad + piece.astype(jnp.bfloat16).astype(jnp.float32)
        input_token_rows = (frozen_input_grad + adapter_input_grad.astype(jnp.float32)).astype(jnp.bfloat16)
        down_outer_product = adapter_scale * up_reduced.astype(jnp.float32)[:, :, None] * input_rows_local.astype(jnp.float32)[:, None, :]
        up_outer_product = adapter_scale * down_reduced.astype(jnp.float32)[:, :, None] * gradient_rows.astype(jnp.float32)[:, None, :]
        grad_down = grad_down + jax.ops.segment_sum(down_outer_product, tok_slot, num_segments=ADAPTER_TOTAL)
        grad_up = grad_up + jax.ops.segment_sum(up_outer_product, tok_slot, num_segments=ADAPTER_TOTAL)
        return (grad_down, grad_up), input_token_rows

    start = (jnp.zeros((ADAPTER_TOTAL, ADAPTER_RANK, INPUT_FEATURES), jnp.float32), jnp.zeros((ADAPTER_TOTAL, ADAPTER_RANK, OUTPUT_FEATURES), jnp.float32))
    (grad_down, grad_up), rows = lax.scan(device_step, start, jnp.arange(N_ADAPTER, dtype=jnp.int32))
    return rows.reshape(TOKENS, INPUT_FEATURES), grad_down.reshape(ADAPTER_TOTAL * ADAPTER_RANK, INPUT_FEATURES), grad_up.reshape(ADAPTER_TOTAL * ADAPTER_RANK, OUTPUT_FEATURES)
```

```python
import functools

import jax
import jax.numpy as jnp
from jax import lax
from jax.experimental import pallas as pl
from jax.experimental.pallas import tpu as pltpu
from jax.sharding import PartitionSpec as P

MESH = pl.DeviceIdType.MESH
F32 = jnp.float32
BF16 = jnp.bfloat16
RANK = 16
SLOTS = 8
NX, NZ, NC, NY = 4, 8, 2, 4
PLANE = NX * NC
CAP = 16
ROWS = PLANE * CAP
HALF = ROWS // 2
PEERS = ((2, 0), (2, 1), (1, 0), (1, 1), (3, 0), (3, 1), (0, 1))
DIRS = (1, NZ - 1)
HOPS = NZ // 2

NT = (((1,), (1,)), ((), ()))
NN = (((1,), (0,)), ((), ()))


def mm(a, b, dims=NN):
    return lax.dot_general(a, b, dims, preferred_element_type=F32)


def iota(shape, dim):
    return lax.broadcasted_iota(jnp.int32, shape, dim)


def kernel(
    x_hbm, g_hbm, w_hbm, ad_hbm, bu_hbm, table_ref, gai_ref, len_ref,
    dx_ref, dgrad_ref, ugrad_ref,
    xv, gv, wv, xp, gp, tokx, tokg, aga, agb, meta_s, meta_r, masks,
    low_s, low_r, wide, wide_t, base_s, base_r, lora_s, lora_r, rs_s, rs_r, idx_row, idx_col,
    local_sem, x_send, x_recv, ag_send, ag_recv, rs_send, rs_recv, low_send, low_recv, base_send, base_recv,
):
    me = lax.axis_index("adapter")
    y = lax.axis_index("tensor")
    x = lax.div(me, NZ * NC)
    z = lax.rem(lax.div(me, NC), NZ)
    c = lax.rem(me, NC)
    p = x * NC + c

    def at(xx, zz, cc):
        return (xx * NZ + zz) * NC + cc

    def zplus(d):
        return lax.rem(z + (d + 2 * NZ), NZ)

    def column(k):
        dx, dc = k
        return lax.rem(x + dx, NX), lax.rem(c + dc, NC)

    def column_from(k):
        dx, dc = k
        return lax.rem(x + (NX - dx), NX), lax.rem(c + dc, NC)

    locals_ = {
        "g": pltpu.make_async_copy(g_hbm, gv, local_sem.at[0]),
        "x": pltpu.make_async_copy(x_hbm, xv, local_sem.at[1]),
        "b": pltpu.make_async_copy(bu_hbm, agb.at[z], local_sem.at[2]),
        "a": pltpu.make_async_copy(ad_hbm, aga.at[z], local_sem.at[3]),
        "w": pltpu.make_async_copy(w_hbm, wv, local_sem.at[4]),
    }

    def plane_copy(unit, i, src, dst):
        xx, cc = column(PEERS[i])
        return pltpu.make_async_remote_copy(
            src_ref=src, dst_ref=dst, send_sem=x_send.at[unit, i], recv_sem=x_recv.at[unit, i],
            device_id=(at(xx, z, cc), y), device_id_type=MESH,
        )

    def token_copy(unit, i):
        packed, landed = ((gp, tokg), (xp, tokx))[unit]
        xx, cc = column(PEERS[i])
        return plane_copy(unit, i, packed.at[xx * NC + cc], landed.at[:, p])

    def meta_copy(i):
        xx, cc = column(PEERS[i])
        return plane_copy(3, i, meta_s.at[xx * NC + cc], meta_r.at[p])

    def lora_copy(i):
        xx, cc = column(PEERS[i])
        return plane_copy(2, i, lora_s.at[:, xx * NC + cc], lora_r.at[p])

    def ag_copy(u, d, h, f):
        own = (bu_hbm, ad_hbm)[u]
        buf = (agb, aga)[u]
        rows = pl.ds(f * HALF, HALF)
        source = zplus(-(h - 1) if d == 0 else h - 1)
        src = own.at[rows] if h == 1 else buf.at[source, rows]
        return pltpu.make_async_remote_copy(
            src_ref=src, dst_ref=buf.at[source, rows],
            send_sem=ag_send.at[u, d, h - 1, f], recv_sem=ag_recv.at[u, d, h - 1, f],
            device_id=(at(x, zplus(DIRS[d]), c), y), device_id_type=MESH,
        )

    def rs_copy(u, d, h, f):
        return pltpu.make_async_remote_copy(
            src_ref=rs_s.at[u, d, h - 1, f], dst_ref=rs_r.at[u, d, h - 1, f],
            send_sem=rs_send.at[u, d, h - 1, f], recv_sem=rs_recv.at[u, d, h - 1, f],
            device_id=(at(x, zplus(DIRS[d]), c), y), device_id_type=MESH,
        )

    def low_copy(u, dy):
        return pltpu.make_async_remote_copy(
            src_ref=low_s.at[u], dst_ref=low_r.at[u, dy - 1],
            send_sem=low_send.at[u, dy - 1], recv_sem=low_recv.at[u, dy - 1],
            device_id=(me, lax.rem(y + dy, NY)), device_id_type=MESH,
        )

    def base_copy(dy):
        return pltpu.make_async_remote_copy(
            src_ref=base_s.at[dy], dst_ref=base_r.at[dy - 1],
            send_sem=base_send.at[dy - 1], recv_sem=base_recv.at[dy - 1],
            device_id=(me, lax.rem(y + dy, NY)), device_id_type=MESH,
        )

    def halves(h):
        return [(d, f) for f in (0, 1) for d in (0, 1) if h < HOPS or f == d]

    for name in ("g", "b", "x", "w", "a"):
        locals_[name].start()
    barrier = pltpu.get_barrier_semaphore()
    partners = [(at(*_xzc(column(k), z)), y) for k in PEERS]
    partners += [(at(x, zplus(d), c), y) for d in DIRS]
    partners += [(me, lax.rem(y + dy, NY)) for dy in range(1, NY)]
    for partner in partners:
        pl.semaphore_signal(barrier, inc=1, device_id=partner, device_id_type=MESH)

    ng = gai_ref.shape[1]
    toks = gv.shape[0]
    eye = iota((ng, ng), 0) == iota((ng, ng), 1)

    def to_col(row):
        return jnp.sum(jnp.where(eye, row, 0.0), axis=1, keepdims=True)

    def to_row(col):
        return jnp.sum(jnp.where(eye, col, 0.0), axis=0, keepdims=True)

    gai_col = to_col(gai_ref[...].astype(F32)).astype(jnp.int32)
    len_row = len_ref[...].astype(F32)
    len_col = to_col(len_row)
    n_adapters = table_ref.shape[1]
    slot = jnp.sum(
        jnp.where(iota((ng, n_adapters), 1) == gai_col, table_ref[...].astype(F32), 0.0), axis=1, keepdims=True
    ).astype(jnp.int32)
    local = slot & (SLOTS - 1)
    owner_c = (slot >> 3) & 1
    owner_z = (slot >> 4) & (NZ - 1)
    owner_x = slot >> 7
    pair = (owner_x * NC + owner_c) * NZ + owner_z
    start = jnp.sum(jnp.where(iota((ng, ng), 1) < iota((ng, ng), 0), len_row, 0.0), axis=1, keepdims=True)
    shift = (pair * CAP).astype(F32) - start
    end = start + len_col
    t_row = iota((ng, toks), 1).astype(F32)
    idx_row[...] = jnp.sum(
        jnp.where((t_row >= start) & (t_row < end), shift + t_row, 0.0), axis=0, keepdims=True
    ).astype(jnp.int32)
    t_col = iota((toks, ng), 0).astype(F32)
    idx_col[...] = jnp.sum(
        jnp.where((t_col >= to_row(start)) & (t_col < to_row(end)), to_row(shift) + t_col, 0.0), axis=1, keepdims=True
    ).astype(jnp.int32)
    pairs = PLANE * NZ
    slot_of_pair = jnp.sum(
        jnp.where(iota((pairs, ng), 0) == to_row(pair.astype(F32)).astype(jnp.int32), to_row(local.astype(F32)) + 1.0, 0.0),
        axis=1, keepdims=True,
    ).astype(jnp.int32)
    mask = jnp.where((iota((pairs, ROWS), 1) >> 4) + 1 == slot_of_pair, 1.0, 0.0)
    meta_s[...] = mask.reshape(PLANE, NZ, ROWS)
    meta_r[pl.ds(p, 1)] = meta_s[pl.ds(p, 1)]

    pl.semaphore_wait(barrier, len(partners))

    for d, f in halves(1):
        ag_copy(0, d, 1, f).start()
    for i in range(len(PEERS)):
        meta_copy(i).start()

    def pack(source, packed, q):
        hot = jnp.where(iota((ROWS, toks), 0) + q * ROWS == idx_row[...], 1.0, 0.0).astype(BF16)
        packed[q] = mm(hot, source[...]).astype(BF16).reshape(NZ, CAP, -1)

    def forward(u, h):
        for d, f in halves(h):
            source = zplus(-h if d == 0 else h)
            buf = (agb, aga)[u]
            landed = buf.at[source, pl.ds(f * HALF, HALF)]
            pltpu.make_async_remote_copy(
                src_ref=landed, dst_ref=landed, send_sem=ag_send.at[u, d, h - 1, f],
                recv_sem=ag_recv.at[u, d, h - 1, f], device_id=(at(x, zplus(DIRS[d]), c), y), device_id_type=MESH,
            ).wait_recv()
            if h < HOPS and (d, f) in halves(h + 1):
                ag_copy(u, d, h + 1, f).start()

    def base_block(dy):
        block = lax.rem(y + dy, NY)
        width = 256

        def tile(n, carry):
            rows = pl.ds(pl.multiple_of(block * wv.shape[1] + n * width, width), width)
            cols = pl.ds(pl.multiple_of(n * width, width), width)
            base_s[dy, :, cols] = mm(gv[...], wv[rows, :], NT).astype(BF16)
            return carry

        lax.fori_loop(0, wv.shape[1] // width, tile, 0)

    def select(zt, transposed):
        a, b = iota((ROWS, ROWS), 0), iota((ROWS, ROWS), 1)
        narrow, broad = (a, b) if transposed else (b, a)
        return jnp.where(narrow == zt * RANK + (broad & (RANK - 1)), 1.0, 0.0).astype(BF16)

    def project(u, tok, weights):
        def block(zt, acc):
            wide_p = mm(tok[zt].reshape(ROWS, -1), weights[zt], NT) * masks[zt]
            return acc + mm(wide_p.astype(BF16), select(zt, False))

        acc = lax.fori_loop(0, NZ, block, jnp.zeros((ROWS, ROWS), F32))
        low_s[u] = acc.astype(BF16)
        for dy in (2, 1, 3):
            low_copy(u, dy).start()

    def spread(u):
        total = low_s[u].astype(F32)
        for dy in range(1, NY):
            low_copy(u, dy).wait_recv()
            total = total + low_r[u, dy - 1].astype(F32)
        low = total.astype(BF16)

        def block(zt, carry):
            twice = mm(low, select(zt, True)) * (2.0 * masks[zt])
            if u == 0:
                wide[zt] = twice.astype(BF16)
            wide_t[u, zt] = twice.T.astype(BF16)
            return carry

        lax.fori_loop(0, NZ, block, 0)

    def lora(zt):
        lora_s[zt] = mm(wide[zt], aga[zt]).astype(BF16).reshape(PLANE, CAP, -1)

    toks_of = (tokx, tokg)

    def term(u, zt, f):
        return mm(wide_t[u, zt, f * HALF : (f + 1) * HALF, :], toks_of[u][zt].reshape(ROWS, -1))

    def rs_target(d, h):
        return zplus((HOPS + 1 - h) if d == 0 else -(HOPS + 1 - h))

    def rs_init(u):
        for h in (1, 2):
            for d in (0, 1):
                f = d if h == 1 else 1 - d
                rs_s[u, d, h - 1, f] = term(u, rs_target(d, h), f).astype(BF16)
                rs_copy(u, d, h, f).start()

    def rs_step(u, h):
        for f in (0, 1):
            for d in (0, 1):
                if h == 1 and f != d:
                    continue
                rs_copy(u, d, h, f).wait_recv()
                total = rs_r[u, d, h - 1, f].astype(F32) + term(u, rs_target(d, h + 1), f)
                rs_s[u, d, h, f] = total.astype(BF16)
                rs_copy(u, d, h + 1, f).start()

    def rs_last(u):
        out = (dgrad_ref, ugrad_ref)[u]
        for f in (0, 1):
            total = term(u, z, f)
            for d in (0, 1):
                rs_copy(u, d, HOPS, f).wait_recv()
                total = total + rs_r[u, d, HOPS - 1, f].astype(F32)
            out[f * HALF : (f + 1) * HALF, :] = total

    locals_["g"].wait()
    for i, k in enumerate(PEERS):
        xx, cc = column(k)
        pack(gv, gp, xx * NC + cc)
        token_copy(0, i).start()
    locals_["w"].wait()
    base_block(2)
    base_copy(2).start()
    forward(0, 1)
    base_block(1)
    base_copy(1).start()
    base_block(3)
    base_copy(3).start()
    pack(gv, gp, p)
    tokg[:, pl.ds(p, 1)] = gp[pl.ds(p, 1)].reshape(NZ, 1, CAP, -1)
    forward(0, 2)
    locals_["x"].wait()
    for i, k in enumerate(PEERS):
        xx, cc = column(k)
        pack(xv, xp, xx * NC + cc)
    pack(xv, xp, p)
    tokx[:, pl.ds(p, 1)] = xp[pl.ds(p, 1)].reshape(NZ, 1, CAP, -1)
    forward(0, 3)
    for d, f in halves(1):
        ag_copy(1, d, 1, f).start()
    for i in range(len(PEERS)):
        token_copy(1, i).start()
    for i in range(len(PEERS)):
        meta_copy(i).wait_recv()
    for zt in range(NZ):
        masks[zt] = jnp.broadcast_to(meta_r[:, zt : zt + 1, :], (PLANE, CAP, ROWS)).reshape(ROWS, ROWS)
    base_block(0)
    forward(0, HOPS)
    locals_["b"].wait()
    for i in range(len(PEERS)):
        token_copy(0, i).wait_recv()
    project(0, tokg, agb)
    forward(1, 1)
    spread(0)
    locals_["a"].wait()
    lora(z)
    lora(zplus(1))
    lora(zplus(-1))
    forward(1, 2)
    lora(zplus(2))
    lora(zplus(-2))
    forward(1, 3)
    lora(zplus(3))
    lora(zplus(-3))
    forward(1, HOPS)
    lora(zplus(HOPS))
    for i in range(len(PEERS)):
        lora_copy(i).start()
    lora_r[pl.ds(p, 1)] = lora_s[:, pl.ds(p, 1)].reshape(1, NZ, CAP, -1)
    for i in range(len(PEERS)):
        token_copy(1, i).wait_recv()
    rs_init(0)
    project(1, tokx, aga)
    rs_step(0, 1)
    spread(1)
    rs_step(0, 2)
    rs_step(0, 3)
    rs_init(1)
    rs_last(0)
    rs_step(1, 1)
    for dy in range(1, NY):
        base_copy(dy).wait_recv()
    for i in range(len(PEERS)):
        lora_copy(i).wait_recv()
    rs_step(1, 2)

    def finish(n, carry):
        rows = pl.ds(pl.multiple_of(n * ROWS, ROWS), ROWS)
        hot = jnp.where(iota((ROWS, PLANE * ROWS), 1) == idx_col[rows, :], 1.0, 0.0).astype(BF16)
        total = mm(hot, lora_r[...].reshape(PLANE * ROWS, -1)) + base_s[0, rows, :].astype(F32)
        for dy in range(1, NY):
            total = total + base_r[dy - 1, rows, :].astype(F32)
        dx_ref[rows, :] = total.astype(BF16)
        return carry

    lax.fori_loop(0, 2, finish, 0)
    rs_step(1, 3)
    lax.fori_loop(2, toks // ROWS, finish, 0)
    rs_last(1)

    for i in range(len(PEERS)):
        meta_copy(i).wait_send()
        token_copy(0, i).wait_send()
        token_copy(1, i).wait_send()
        lora_copy(i).wait_send()
    for u in (0, 1):
        for h in range(1, HOPS + 1):
            for d, f in halves(h):
                ag_copy(u, d, h, f).wait_send()
            for f in (0, 1):
                for d in (0, 1):
                    if h > 1 or f == d:
                        rs_copy(u, d, h, f).wait_send()
        for dy in range(1, NY):
            low_copy(u, dy).wait_send()
    for dy in range(1, NY):
        base_copy(dy).wait_send()


def _xzc(xc, z):
    return xc[0], z, xc[1]


def on_device(
    activations,
    output_gradient,
    frozen_weight,
    adapter_down_weight,
    adapter_up_weight,
    adapter_slot_table,
    group_adapter_index,
    group_token_length,
):
    toks, feats = activations.shape
    own = adapter_down_weight.shape[0]
    any_spec = pl.BlockSpec(memory_space=pl.ANY)
    vmem_spec = pl.BlockSpec(memory_space=pltpu.VMEM)
    dma = pltpu.SemaphoreType.DMA
    n = len(PEERS)
    return pl.pallas_call(
        kernel,
        out_shape=(
            jax.ShapeDtypeStruct((toks, feats), BF16),
            jax.ShapeDtypeStruct((own, feats), F32),
            jax.ShapeDtypeStruct((own, feats), F32),
        ),
        in_specs=[any_spec] * 5 + [vmem_spec] * 3,
        out_specs=(vmem_spec,) * 3,
        scratch_shapes=[
            pltpu.VMEM((toks, feats), BF16),
            pltpu.VMEM((toks, feats), BF16),
            pltpu.VMEM(frozen_weight.shape, BF16),
            pltpu.VMEM((PLANE, NZ, CAP, feats), BF16),
            pltpu.VMEM((PLANE, NZ, CAP, feats), BF16),
            pltpu.VMEM((NZ, PLANE, CAP, feats), BF16),
            pltpu.VMEM((NZ, PLANE, CAP, feats), BF16),
            pltpu.VMEM((NZ, ROWS, feats), BF16),
            pltpu.VMEM((NZ, ROWS, feats), BF16),
            pltpu.VMEM((PLANE, NZ, ROWS), F32),
            pltpu.VMEM((PLANE, NZ, ROWS), F32),
            pltpu.VMEM((NZ, ROWS, ROWS), F32),
            pltpu.VMEM((2, ROWS, ROWS), BF16),
            pltpu.VMEM((2, NY - 1, ROWS, ROWS), BF16),
            pltpu.VMEM((NZ, ROWS, ROWS), BF16),
            pltpu.VMEM((2, NZ, ROWS, ROWS), BF16),
            pltpu.VMEM((NY, toks, feats), BF16),
            pltpu.VMEM((NY - 1, toks, feats), BF16),
            pltpu.VMEM((NZ, PLANE, CAP, feats), BF16),
            pltpu.VMEM((PLANE, NZ, CAP, feats), BF16),
            pltpu.VMEM((2, 2, HOPS, 2, HALF, feats), BF16),
            pltpu.VMEM((2, 2, HOPS, 2, HALF, feats), BF16),
            pltpu.VMEM((1, toks), jnp.int32),
            pltpu.VMEM((toks, 1), jnp.int32),
            dma((5,)),
            dma((4, n)),
            dma((4, n)),
            dma((2, 2, HOPS, 2)),
            dma((2, 2, HOPS, 2)),
            dma((2, 2, HOPS, 2)),
            dma((2, 2, HOPS, 2)),
            dma((2, NY - 1)),
            dma((2, NY - 1)),
            dma((NY - 1,)),
            dma((NY - 1,)),
        ],
        compiler_params=pltpu.CompilerParams(
            collective_id=0, has_side_effects=True, vmem_limit_bytes=60 * 1024 * 1024
        ),
        name="lora_backward",
    )(
        activations,
        output_gradient,
        frozen_weight,
        adapter_down_weight,
        adapter_up_weight,
        adapter_slot_table.reshape(1, -1),
        group_adapter_index,
        group_token_length,
    )


def solution(mesh):
    in_specs = (
        P("adapter", "tensor"),
        P("adapter", "tensor"),
        P(None, "tensor"),
        P("adapter", "tensor"),
        P("adapter", "tensor"),
        P(),
        P("adapter", None),
        P("adapter", None),
    )
    out_specs = (P("adapter", "tensor"), P("adapter", "tensor"), P("adapter", "tensor"))
    return jax.shard_map(
        on_device, mesh=mesh, in_specs=in_specs, out_specs=out_specs, check_vma=False
    )
```

```python
import functools

import jax
import jax.numpy as jnp
from jax import lax
from jax.experimental import pallas as pl
from jax.experimental.pallas import tpu as pltpu
from jax.sharding import PartitionSpec as P

MESH = pl.DeviceIdType.MESH
F32 = jnp.float32
BF16 = jnp.bfloat16
RANK = 16
SLOTS = 8
NX, NZ, NC, NY = 4, 8, 2, 4
PLANE = NX * NC
CAP = 16
ROWS = PLANE * CAP
HALF = ROWS // 2
PEERS = ((2, 0), (2, 1), (1, 0), (1, 1), (3, 0), (3, 1), (0, 1))
DIRS = (1, NZ - 1)
FIRST, SECOND = ((0, 0), (1, 1)), ((0, 1), (1, 0))
NEAR = NZ // 2
HOPS = NZ // 2

NT = (((1,), (1,)), ((), ()))
NN = (((1,), (0,)), ((), ()))


def mm(a, b, dims=NN):
    return lax.dot_general(a, b, dims, preferred_element_type=F32)


def iota(shape, dim):
    return lax.broadcasted_iota(jnp.int32, shape, dim)


def kernel(
    x_hbm, g_hbm, w_hbm, ad_hbm, bu_hbm, table_ref, gai_ref, len_ref,
    dx_ref, dgrad_ref, ugrad_ref,
    xv, gv, wv, xp, gp, tokx, tokg, aga, agb, meta_s, meta_r, masks,
    low_acc, low_s, low_r, wide, wide_t, base_s, base_r, lora_s, lora_r, rs_s, rs_r, idx_row, idx_col,
    local_sem, x_send, x_recv, ag_send, ag_recv, rs_send, rs_recv, low_send, low_recv, base_send, base_recv,
):
    toks = gv.shape[0]
    me = lax.axis_index("adapter")
    y = lax.axis_index("tensor")
    x = lax.div(me, NZ * NC)
    z = lax.rem(lax.div(me, NC), NZ)
    c = lax.rem(me, NC)
    p = x * NC + c

    def at(xx, zz, cc):
        return (xx * NZ + zz) * NC + cc

    def zplus(d):
        return lax.rem(z + (d + 2 * NZ), NZ)

    def column(k):
        dx, dc = k
        return lax.rem(x + dx, NX), lax.rem(c + dc, NC)

    def owner_z_of(e):
        return zplus(e + 2)

    locals_ = {
        "g": pltpu.make_async_copy(g_hbm, gv, local_sem.at[0]),
        "x": pltpu.make_async_copy(x_hbm, xv, local_sem.at[1]),
        "b": pltpu.make_async_copy(bu_hbm, agb.at[z], local_sem.at[2]),
        "a": pltpu.make_async_copy(ad_hbm, aga.at[z], local_sem.at[3]),
        "w": pltpu.make_async_copy(w_hbm, wv, local_sem.at[4]),
    }

    def plane_copy(unit, i, src, dst):
        xx, cc = column(PEERS[i])
        return pltpu.make_async_remote_copy(
            src_ref=src, dst_ref=dst, send_sem=x_send.at[unit, i], recv_sem=x_recv.at[unit, i],
            device_id=(at(xx, z, cc), y), device_id_type=MESH,
        )

    def token_copy(unit, i):
        packed, landed, first, count = ((gp, tokg, 0, NZ), (xp, tokx, 0, NEAR), (xp, tokx, NEAR, NZ - NEAR))[unit]
        xx, cc = column(PEERS[i])
        entries = pl.ds(first, count)
        return plane_copy(unit, i, packed.at[xx * NC + cc, entries], landed.at[entries, p])

    def meta_copy(i):
        xx, cc = column(PEERS[i])
        return plane_copy(4, i, meta_s.at[xx * NC + cc], meta_r.at[p])

    def lora_copy(i):
        xx, cc = column(PEERS[i])
        return plane_copy(3, i, lora_s.at[:, xx * NC + cc], lora_r.at[p])

    def ag_copy(u, d, h, f):
        own = (bu_hbm, ad_hbm)[u]
        buf = (agb, aga)[u]
        rows = pl.ds(f * HALF, HALF)
        source = zplus(-(h - 1) if d == 0 else h - 1)
        src = own.at[rows] if h == 1 else buf.at[source, rows]
        return pltpu.make_async_remote_copy(
            src_ref=src, dst_ref=buf.at[source, rows],
            send_sem=ag_send.at[u, d, h - 1, f], recv_sem=ag_recv.at[u, d, h - 1, f],
            device_id=(at(x, zplus(DIRS[d]), c), y), device_id_type=MESH,
        )

    def rs_copy(u, d, h, f):
        return pltpu.make_async_remote_copy(
            src_ref=rs_s.at[u, d, h - 1, f], dst_ref=rs_r.at[u, d, h - 1, f],
            send_sem=rs_send.at[u, d, h - 1, f], recv_sem=rs_recv.at[u, d, h - 1, f],
            device_id=(at(x, zplus(DIRS[d]), c), y), device_id_type=MESH,
        )

    def low_copy(u, dy):
        return pltpu.make_async_remote_copy(
            src_ref=low_s.at[u], dst_ref=low_r.at[u, dy - 1],
            send_sem=low_send.at[u, dy - 1], recv_sem=low_recv.at[u, dy - 1],
            device_id=(me, lax.rem(y + dy, NY)), device_id_type=MESH,
        )

    def base_copy(dy, f):
        rows = pl.ds(f * (toks // 2), toks // 2)
        return pltpu.make_async_remote_copy(
            src_ref=base_s.at[dy, rows], dst_ref=base_r.at[dy - 1, rows],
            send_sem=base_send.at[dy - 1, f], recv_sem=base_recv.at[dy - 1, f],
            device_id=(me, lax.rem(y + dy, NY)), device_id_type=MESH,
        )

    def halves(h):
        return FIRST + SECOND if h < HOPS else FIRST

    for name in ("g", "b", "x", "w", "a"):
        locals_[name].start()
    barrier = pltpu.get_barrier_semaphore()
    partners = [(at(*_xzc(column(k), z)), y) for k in PEERS]
    partners += [(at(x, zplus(d), c), y) for d in DIRS]
    partners += [(me, lax.rem(y + dy, NY)) for dy in range(1, NY)]
    for partner in partners:
        pl.semaphore_signal(barrier, inc=1, device_id=partner, device_id_type=MESH)

    ng = gai_ref.shape[1]
    eye = iota((ng, ng), 0) == iota((ng, ng), 1)

    def to_col(row):
        return jnp.sum(jnp.where(eye, row, 0.0), axis=1, keepdims=True)

    def to_row(col):
        return jnp.sum(jnp.where(eye, col, 0.0), axis=0, keepdims=True)

    gai_col = to_col(gai_ref[...].astype(F32)).astype(jnp.int32)
    len_row = len_ref[...].astype(F32)
    len_col = to_col(len_row)
    n_adapters = table_ref.shape[1]
    slot = jnp.sum(
        jnp.where(iota((ng, n_adapters), 1) == gai_col, table_ref[...].astype(F32), 0.0), axis=1, keepdims=True
    ).astype(jnp.int32)
    local = slot & (SLOTS - 1)
    owner_c = (slot >> 3) & 1
    owner_z = (slot >> 4) & (NZ - 1)
    owner_x = slot >> 7
    pair = (owner_x * NC + owner_c) * NZ + ((owner_z + (NZ - 2) + (NZ - z)) & (NZ - 1))
    start = jnp.sum(jnp.where(iota((ng, ng), 1) < iota((ng, ng), 0), len_row, 0.0), axis=1, keepdims=True)
    shift = (pair * CAP).astype(F32) - start
    end = start + len_col
    t_row = iota((ng, toks), 1).astype(F32)
    idx_row[...] = jnp.sum(
        jnp.where((t_row >= start) & (t_row < end), shift + t_row, 0.0), axis=0, keepdims=True
    ).astype(jnp.int32)
    t_col = iota((toks, ng), 0).astype(F32)
    idx_col[...] = jnp.sum(
        jnp.where((t_col >= to_row(start)) & (t_col < to_row(end)), to_row(shift) + t_col, 0.0), axis=1, keepdims=True
    ).astype(jnp.int32)
    pairs = PLANE * NZ
    slot_of_pair = jnp.sum(
        jnp.where(iota((pairs, ng), 0) == to_row(pair.astype(F32)).astype(jnp.int32), to_row(local.astype(F32)) + 1.0, 0.0),
        axis=1, keepdims=True,
    ).astype(jnp.int32)
    mask = jnp.where((iota((pairs, ROWS), 1) >> 4) + 1 == slot_of_pair, 1.0, 0.0)
    meta_s[...] = mask.reshape(PLANE, NZ, ROWS)
    meta_r[pl.ds(p, 1)] = meta_s[pl.ds(p, 1)]

    pl.semaphore_wait(barrier, len(partners))

    for d, f in halves(1):
        ag_copy(0, d, 1, f).start()
    for i in range(len(PEERS)):
        meta_copy(i).start()

    def pack(source, packed, q):
        hot = jnp.where(iota((ROWS, toks), 0) + q * ROWS == idx_row[...], 1.0, 0.0).astype(BF16)
        packed[q] = mm(hot, source[...]).astype(BF16).reshape(NZ, CAP, -1)

    def forward(u, h, part):
        for d, f in part:
            source = zplus(-h if d == 0 else h)
            buf = (agb, aga)[u]
            landed = buf.at[source, pl.ds(f * HALF, HALF)]
            pltpu.make_async_remote_copy(
                src_ref=landed, dst_ref=landed, send_sem=ag_send.at[u, d, h - 1, f],
                recv_sem=ag_recv.at[u, d, h - 1, f], device_id=(at(x, zplus(DIRS[d]), c), y), device_id_type=MESH,
            ).wait_recv()
            if h < HOPS and (d, f) in halves(h + 1):
                ag_copy(u, d, h + 1, f).start()

    def base_block(dy):
        block = lax.rem(y + dy, NY)
        width = 256

        def tile(n, carry):
            rows = pl.ds(pl.multiple_of(block * wv.shape[1] + n * width, width), width)
            cols = pl.ds(pl.multiple_of(n * width, width), width)
            base_s[dy, :, cols] = mm(gv[...], wv[rows, :], NT).astype(BF16)
            return carry

        lax.fori_loop(0, wv.shape[1] // width, tile, 0)

    def select(e, transposed):
        a, b = iota((ROWS, ROWS), 0), iota((ROWS, ROWS), 1)
        narrow, broad = (a, b) if transposed else (b, a)
        return jnp.where(narrow == e * RANK + (broad & (RANK - 1)), 1.0, 0.0).astype(BF16)

    toks_of = (tokx, tokg)
    project_of = (tokg, tokx)
    maps_of = (agb, aga)

    def project(u, first, count):
        def block(e, carry):
            wide_p = mm(project_of[u][e].reshape(ROWS, -1), maps_of[u][owner_z_of(e)], NT) * masks[e]
            part_low = mm(wide_p.astype(BF16), select(e, False))
            low_acc[...] = jnp.where(e == 0, part_low, low_acc[...] + part_low)
            return carry

        lax.fori_loop(first, first + count, block, 0)

    def low_sends(u):
        low_s[u] = low_acc[...].astype(BF16)
        for dy in (2, 1, 3):
            low_copy(u, dy).start()

    def spread(u):
        total = low_s[u].astype(F32)
        for dy in range(1, NY):
            low_copy(u, dy).wait_recv()
            total = total + low_r[u, dy - 1].astype(F32)
        low = total.astype(BF16)

        def block(e, carry):
            twice = mm(low, select(e, True)) * (2.0 * masks[e])
            if u == 0:
                wide[e] = twice.astype(BF16)
            wide_t[u, e] = twice.T.astype(BF16)
            return carry

        lax.fori_loop(0, NZ, block, 0)

    def lora(distance):
        e = (distance - 2) % NZ
        lora_s[e] = mm(wide[e], aga[zplus(distance)]).astype(BF16).reshape(PLANE, CAP, -1)

    def term(u, distance, f):
        e = (distance - 2) % NZ
        return mm(wide_t[u, e, f * HALF : (f + 1) * HALF, :], toks_of[u][e].reshape(ROWS, -1))

    def rs_target(d, h):
        return (HOPS + 1 - h) if d == 0 else -(HOPS + 1 - h)

    def rs_init(u):
        for h, part in ((1, FIRST), (2, SECOND)):
            for d, f in part:
                rs_s[u, d, h - 1, f] = term(u, rs_target(d, h), f).astype(BF16)
                rs_copy(u, d, h, f).start()

    def rs_step(u, h, part):
        for d, f in part:
            rs_copy(u, d, h, f).wait_recv()
            total = rs_r[u, d, h - 1, f].astype(F32) + term(u, rs_target(d, h + 1), f)
            rs_s[u, d, h, f] = total.astype(BF16)
            rs_copy(u, d, h + 1, f).start()

    def rs_last(u):
        out = (dgrad_ref, ugrad_ref)[u]
        own = [term(u, 0, f) for f in (0, 1)]
        for d, f in SECOND:
            rs_copy(u, d, HOPS, f).wait_recv()
            own[f] = own[f] + rs_r[u, d, HOPS - 1, f].astype(F32)
        for d, f in FIRST:
            rs_copy(u, d, HOPS, f).wait_recv()
            out[f * HALF : (f + 1) * HALF, :] = own[f] + rs_r[u, d, HOPS - 1, f].astype(F32)

    def finish(n, carry):
        rows = pl.ds(pl.multiple_of(n * ROWS, ROWS), ROWS)
        hot = jnp.where(iota((ROWS, PLANE * ROWS), 1) == idx_col[rows, :], 1.0, 0.0).astype(BF16)
        total = mm(hot, lora_r[...].reshape(PLANE * ROWS, -1)) + base_s[0, rows, :].astype(F32)
        for dy in range(1, NY):
            total = total + base_r[dy - 1, rows, :].astype(F32)
        dx_ref[rows, :] = total.astype(BF16)
        return carry

    def own_tokens(packed, landed):
        pack(gv if packed is gp else xv, packed, p)
        landed[:, pl.ds(p, 1)] = packed[pl.ds(p, 1)].reshape(NZ, 1, CAP, -1)

    every = range(len(PEERS))
    locals_["g"].wait()
    for i in every:
        xx, cc = column(PEERS[i])
        pack(gv, gp, xx * NC + cc)
        token_copy(0, i).start()
    forward(0, 1, FIRST)
    locals_["w"].wait()
    base_block(1)
    for f in (0, 1):
        base_copy(1, f).start()
    forward(0, 1, SECOND)
    base_block(3)
    for f in (0, 1):
        base_copy(3, f).start()
    forward(0, 2, FIRST)
    locals_["x"].wait()
    for i in every[:4]:
        xx, cc = column(PEERS[i])
        pack(xv, xp, xx * NC + cc)
        token_copy(1, i).start()
    forward(0, 2, SECOND)
    for i in every[4:]:
        xx, cc = column(PEERS[i])
        pack(xv, xp, xx * NC + cc)
        token_copy(1, i).start()
    for i in every:
        token_copy(2, i).start()
    forward(0, 3, FIRST)
    for d, f in FIRST:
        ag_copy(1, d, 1, f).start()
    own_tokens(gp, tokg)
    forward(0, 3, SECOND)
    for d, f in SECOND:
        ag_copy(1, d, 1, f).start()
    own_tokens(xp, tokx)
    for i in every:
        meta_copy(i).wait_recv()
    for e in range(NZ):
        masks[e] = jnp.broadcast_to(meta_r[:, e : e + 1, :], (PLANE, CAP, ROWS)).reshape(ROWS, ROWS)
    base_block(2)
    forward(0, HOPS, FIRST)
    locals_["b"].wait()
    forward(1, 1, FIRST)
    for i in every:
        token_copy(0, i).wait_recv()
    project(0, 0, NZ // 2)
    forward(1, 1, SECOND)
    project(0, NZ // 2, NZ // 2)
    low_sends(0)
    base_copy(2, 0).start()
    forward(1, 2, FIRST)
    spread(0)
    forward(1, 2, SECOND)
    locals_["a"].wait()
    for distance in (0, 1, -1, 2, -2):
        lora(distance)
    forward(1, 3, FIRST)
    for i in every:
        token_copy(1, i).wait_recv()
    forward(1, 3, SECOND)
    rs_init(0)
    lora(3)
    lora(-3)
    forward(1, HOPS, FIRST)
    lora(HOPS)
    for i in every:
        lora_copy(i).start()
    lora_r[pl.ds(p, 1)] = lora_s[:, pl.ds(p, 1)].reshape(1, NZ, CAP, -1)
    project(1, 0, NEAR)
    rs_step(0, 1, FIRST)
    for i in every:
        token_copy(2, i).wait_recv()
    rs_step(0, 2, SECOND)
    project(1, NEAR, NZ - NEAR)
    low_sends(1)
    base_copy(2, 1).start()
    rs_step(0, 2, FIRST)
    base_block(0)
    rs_step(0, 3, SECOND)
    spread(1)
    rs_step(0, 3, FIRST)
    rs_init(1)
    rs_last(0)
    rs_step(1, 1, FIRST)
    rs_step(1, 2, SECOND)
    rs_step(1, 2, FIRST)
    for i in every:
        lora_copy(i).wait_recv()
    for f in (0, 1):
        for dy in range(1, NY):
            base_copy(dy, f).wait_recv()
    lax.fori_loop(0, 2, finish, 0)
    rs_step(1, 3, SECOND)
    lax.fori_loop(2, 3, finish, 0)
    rs_step(1, 3, FIRST)
    lax.fori_loop(3, toks // ROWS, finish, 0)
    rs_last(1)

    for i in range(len(PEERS)):
        meta_copy(i).wait_send()
        for unit in range(3):
            token_copy(unit, i).wait_send()
        lora_copy(i).wait_send()
    for u in (0, 1):
        for h in range(1, HOPS + 1):
            for d, f in halves(h):
                ag_copy(u, d, h, f).wait_send()
            for f in (0, 1):
                for d in (0, 1):
                    if h > 1 or f == d:
                        rs_copy(u, d, h, f).wait_send()
        for dy in range(1, NY):
            low_copy(u, dy).wait_send()
    for dy in range(1, NY):
        for f in (0, 1):
            base_copy(dy, f).wait_send()


def _xzc(xc, z):
    return xc[0], z, xc[1]


def emit(*refs):
    copies = [pltpu.make_async_copy(refs[i], refs[3 + i], refs[6].at[i]) for i in range(3)]
    for copy in copies:
        copy.start()
    for copy in copies:
        copy.wait()


def on_device(
    activations,
    output_gradient,
    frozen_weight,
    adapter_down_weight,
    adapter_up_weight,
    adapter_slot_table,
    group_adapter_index,
    group_token_length,
):
    toks, feats = activations.shape
    own = adapter_down_weight.shape[0]
    any_spec = pl.BlockSpec(memory_space=pl.ANY)
    vmem_spec = pl.BlockSpec(memory_space=pltpu.VMEM)
    dma = pltpu.SemaphoreType.DMA
    n = len(PEERS)
    results = pl.pallas_call(
        kernel,
        out_shape=(
            jax.ShapeDtypeStruct((toks, feats), BF16),
            jax.ShapeDtypeStruct((own, feats), F32),
            jax.ShapeDtypeStruct((own, feats), F32),
        ),
        in_specs=[any_spec] * 5 + [vmem_spec] * 3,
        out_specs=(vmem_spec,) * 3,
        scratch_shapes=[
            pltpu.VMEM((toks, feats), BF16),
            pltpu.VMEM((toks, feats), BF16),
            pltpu.VMEM(frozen_weight.shape, BF16),
            pltpu.VMEM((PLANE, NZ, CAP, feats), BF16),
            pltpu.VMEM((PLANE, NZ, CAP, feats), BF16),
            pltpu.VMEM((NZ, PLANE, CAP, feats), BF16),
            pltpu.VMEM((NZ, PLANE, CAP, feats), BF16),
            pltpu.VMEM((NZ, ROWS, feats), BF16),
            pltpu.VMEM((NZ, ROWS, feats), BF16),
            pltpu.VMEM((PLANE, NZ, ROWS), F32),
            pltpu.VMEM((PLANE, NZ, ROWS), F32),
            pltpu.VMEM((NZ, ROWS, ROWS), F32),
            pltpu.VMEM((ROWS, ROWS), F32),
            pltpu.VMEM((2, ROWS, ROWS), BF16),
            pltpu.VMEM((2, NY - 1, ROWS, ROWS), BF16),
            pltpu.VMEM((NZ, ROWS, ROWS), BF16),
            pltpu.VMEM((2, NZ, ROWS, ROWS), BF16),
            pltpu.VMEM((NY, toks, feats), BF16),
            pltpu.VMEM((NY - 1, toks, feats), BF16),
            pltpu.VMEM((NZ, PLANE, CAP, feats), BF16),
            pltpu.VMEM((PLANE, NZ, CAP, feats), BF16),
            pltpu.VMEM((2, 2, HOPS, 2, HALF, feats), BF16),
            pltpu.VMEM((2, 2, HOPS, 2, HALF, feats), BF16),
            pltpu.VMEM((1, toks), jnp.int32),
            pltpu.VMEM((toks, 1), jnp.int32),
            dma((5,)),
            dma((5, n)),
            dma((5, n)),
            dma((2, 2, HOPS, 2)),
            dma((2, 2, HOPS, 2)),
            dma((2, 2, HOPS, 2)),
            dma((2, 2, HOPS, 2)),
            dma((2, NY - 1)),
            dma((2, NY - 1)),
            dma((NY - 1, 2)),
            dma((NY - 1, 2)),
        ],
        compiler_params=pltpu.CompilerParams(
            collective_id=0, has_side_effects=True, vmem_limit_bytes=60 * 1024 * 1024
        ),
        name="lora_backward",
    )(
        activations,
        output_gradient,
        frozen_weight,
        adapter_down_weight,
        adapter_up_weight,
        adapter_slot_table.reshape(1, -1),
        group_adapter_index,
        group_token_length,
    )
    return pl.pallas_call(
        emit,
        out_shape=tuple(jax.ShapeDtypeStruct(r.shape, r.dtype) for r in results),
        in_specs=[any_spec] * 3,
        out_specs=(any_spec,) * 3,
        scratch_shapes=[dma((3,))],
        name="emit",
    )(*results)


def solution(mesh):
    in_specs = (
        P("adapter", "tensor"),
        P("adapter", "tensor"),
        P(None, "tensor"),
        P("adapter", "tensor"),
        P("adapter", "tensor"),
        P(),
        P("adapter", None),
        P("adapter", None),
    )
    out_specs = (P("adapter", "tensor"), P("adapter", "tensor"), P("adapter", "tensor"))
    return jax.shard_map(
        on_device, mesh=mesh, in_specs=in_specs, out_specs=out_specs, check_vma=False
    )
```

```python
import functools

import jax
import jax.numpy as jnp
from jax import lax
from jax.experimental import pallas as pl
from jax.experimental.pallas import tpu as pltpu
from jax.sharding import PartitionSpec as P

MESH = pl.DeviceIdType.MESH
F32 = jnp.float32
BF16 = jnp.bfloat16
RANK = 16
SLOTS = 8
NX, NZ, NC, NY = 4, 8, 2, 4
PLANE = NX * NC
CAP = 16
ROWS = PLANE * CAP
HALF = ROWS // 2
PEERS = ((2, 0), (2, 1), (1, 0), (1, 1), (3, 0), (3, 1), (0, 1))
DIRS = (1, NZ - 1)
FIRST, SECOND = ((0, 0), (1, 1)), ((0, 1), (1, 0))
NEAR = NZ // 2
HOPS = NZ // 2

NT = (((1,), (1,)), ((), ()))
NN = (((1,), (0,)), ((), ()))


def mm(a, b, dims=NN):
    return lax.dot_general(a, b, dims, preferred_element_type=F32)


def iota(shape, dim):
    return lax.broadcasted_iota(jnp.int32, shape, dim)


def kernel(
    x_hbm, g_hbm, w_hbm, ad_hbm, bu_hbm, table_ref, gai_ref, len_ref,
    dx_ref, dgrad_ref, ugrad_ref,
    xv, gv, wv, xp, gp, tokx, tokg, aga, agb, meta_s, meta_r, masks,
    low_acc, low_s, low_r, wide, wide_t, base_s, base_r, lora_s, lora_r, rs_s, rs_r, idx_row, idx_col,
    local_sem, x_send, x_recv, ag_send, ag_recv, rs_send, rs_recv, low_send, low_recv, base_send, base_recv,
):
    toks = gv.shape[0]
    me = lax.axis_index("adapter")
    y = lax.axis_index("tensor")
    x = lax.div(me, NZ * NC)
    z = lax.rem(lax.div(me, NC), NZ)
    c = lax.rem(me, NC)
    p = x * NC + c

    def at(xx, zz, cc):
        return (xx * NZ + zz) * NC + cc

    def zplus(d):
        return lax.rem(z + (d + 2 * NZ), NZ)

    def column(k):
        dx, dc = k
        return lax.rem(x + dx, NX), lax.rem(c + dc, NC)

    def owner_z_of(e):
        return zplus(e + 2)

    locals_ = {
        "g": pltpu.make_async_copy(g_hbm, gv, local_sem.at[0]),
        "x": pltpu.make_async_copy(x_hbm, xv, local_sem.at[1]),
        "b": pltpu.make_async_copy(bu_hbm, agb.at[z], local_sem.at[2]),
        "a": pltpu.make_async_copy(ad_hbm, aga.at[z], local_sem.at[3]),
        "w": pltpu.make_async_copy(w_hbm, wv, local_sem.at[4]),
    }

    def plane_copy(unit, i, src, dst):
        xx, cc = column(PEERS[i])
        return pltpu.make_async_remote_copy(
            src_ref=src, dst_ref=dst, send_sem=x_send.at[unit, i], recv_sem=x_recv.at[unit, i],
            device_id=(at(xx, z, cc), y), device_id_type=MESH,
        )

    def token_copy(unit, i):
        packed, landed, first, count = ((gp, tokg, 0, NZ), (xp, tokx, 0, NEAR), (xp, tokx, NEAR, NZ - NEAR))[unit]
        xx, cc = column(PEERS[i])
        entries = pl.ds(first, count)
        return plane_copy(unit, i, packed.at[xx * NC + cc, entries], landed.at[entries, p])

    def meta_copy(i):
        xx, cc = column(PEERS[i])
        return plane_copy(4, i, meta_s.at[xx * NC + cc], meta_r.at[p])

    def lora_copy(i):
        xx, cc = column(PEERS[i])
        return plane_copy(3, i, lora_s.at[:, xx * NC + cc], lora_r.at[p])

    def ag_copy(u, d, h, f):
        own = (bu_hbm, ad_hbm)[u]
        buf = (agb, aga)[u]
        rows = pl.ds(f * HALF, HALF)
        source = zplus(-(h - 1) if d == 0 else h - 1)
        src = own.at[rows] if h == 1 else buf.at[source, rows]
        return pltpu.make_async_remote_copy(
            src_ref=src, dst_ref=buf.at[source, rows],
            send_sem=ag_send.at[u, d, h - 1, f], recv_sem=ag_recv.at[u, d, h - 1, f],
            device_id=(at(x, zplus(DIRS[d]), c), y), device_id_type=MESH,
        )

    def rs_copy(u, d, h, f):
        return pltpu.make_async_remote_copy(
            src_ref=rs_s.at[u, d, h - 1, f], dst_ref=rs_r.at[u, d, h - 1, f],
            send_sem=rs_send.at[u, d, h - 1, f], recv_sem=rs_recv.at[u, d, h - 1, f],
            device_id=(at(x, zplus(DIRS[d]), c), y), device_id_type=MESH,
        )

    def low_copy(u, dy):
        return pltpu.make_async_remote_copy(
            src_ref=low_s.at[u], dst_ref=low_r.at[u, dy - 1],
            send_sem=low_send.at[u, dy - 1], recv_sem=low_recv.at[u, dy - 1],
            device_id=(me, lax.rem(y + dy, NY)), device_id_type=MESH,
        )

    def base_copy(dy, f):
        rows = pl.ds(f * (toks // 2), toks // 2)
        return pltpu.make_async_remote_copy(
            src_ref=base_s.at[dy, rows], dst_ref=base_r.at[dy - 1, rows],
            send_sem=base_send.at[dy - 1, f], recv_sem=base_recv.at[dy - 1, f],
            device_id=(me, lax.rem(y + dy, NY)), device_id_type=MESH,
        )

    def halves(h):
        return FIRST + SECOND if h < HOPS else FIRST

    for name in ("g", "b", "x", "w", "a"):
        locals_[name].start()
    barrier = pltpu.get_barrier_semaphore()
    partners = [(at(*_xzc(column(k), z)), y) for k in PEERS]
    partners += [(at(x, zplus(d), c), y) for d in DIRS]
    partners += [(me, lax.rem(y + dy, NY)) for dy in range(1, NY)]
    for partner in partners:
        pl.semaphore_signal(barrier, inc=1, device_id=partner, device_id_type=MESH)

    ng = gai_ref.shape[1]
    eye = iota((ng, ng), 0) == iota((ng, ng), 1)

    def to_col(row):
        return jnp.sum(jnp.where(eye, row, 0.0), axis=1, keepdims=True)

    def to_row(col):
        return jnp.sum(jnp.where(eye, col, 0.0), axis=0, keepdims=True)

    gai_col = to_col(gai_ref[...].astype(F32)).astype(jnp.int32)
    len_row = len_ref[...].astype(F32)
    len_col = to_col(len_row)
    n_adapters = table_ref.shape[1]
    slot = jnp.sum(
        jnp.where(iota((ng, n_adapters), 1) == gai_col, table_ref[...].astype(F32), 0.0), axis=1, keepdims=True
    ).astype(jnp.int32)
    local = slot & (SLOTS - 1)
    owner_c = (slot >> 3) & 1
    owner_z = (slot >> 4) & (NZ - 1)
    owner_x = slot >> 7
    pair = (owner_x * NC + owner_c) * NZ + ((owner_z + (NZ - 2) + (NZ - z)) & (NZ - 1))
    start = jnp.sum(jnp.where(iota((ng, ng), 1) < iota((ng, ng), 0), len_row, 0.0), axis=1, keepdims=True)
    shift = (pair * CAP).astype(F32) - start
    end = start + len_col
    t_row = iota((ng, toks), 1).astype(F32)
    idx_row[...] = jnp.sum(
        jnp.where((t_row >= start) & (t_row < end), shift + t_row, 0.0), axis=0, keepdims=True
    ).astype(jnp.int32)
    t_col = iota((toks, ng), 0).astype(F32)
    idx_col[...] = jnp.sum(
        jnp.where((t_col >= to_row(start)) & (t_col < to_row(end)), to_row(shift) + t_col, 0.0), axis=1, keepdims=True
    ).astype(jnp.int32)
    pairs = PLANE * NZ
    slot_of_pair = jnp.sum(
        jnp.where(iota((pairs, ng), 0) == to_row(pair.astype(F32)).astype(jnp.int32), to_row(local.astype(F32)) + 1.0, 0.0),
        axis=1, keepdims=True,
    ).astype(jnp.int32)
    mask = jnp.where((iota((pairs, ROWS), 1) >> 4) + 1 == slot_of_pair, 1.0, 0.0)
    meta_s[...] = mask.reshape(PLANE, NZ, ROWS)
    meta_r[pl.ds(p, 1)] = meta_s[pl.ds(p, 1)]

    pl.semaphore_wait(barrier, len(partners))

    for d, f in halves(1):
        ag_copy(0, d, 1, f).start()
    for i in range(len(PEERS)):
        meta_copy(i).start()

    def pack(source, packed, q):
        hot = jnp.where(iota((ROWS, toks), 0) + q * ROWS == idx_row[...], 1.0, 0.0).astype(BF16)
        packed[q] = mm(hot, source[...]).astype(BF16).reshape(NZ, CAP, -1)

    def forward(u, h, part):
        for d, f in part:
            source = zplus(-h if d == 0 else h)
            buf = (agb, aga)[u]
            landed = buf.at[source, pl.ds(f * HALF, HALF)]
            pltpu.make_async_remote_copy(
                src_ref=landed, dst_ref=landed, send_sem=ag_send.at[u, d, h - 1, f],
                recv_sem=ag_recv.at[u, d, h - 1, f], device_id=(at(x, zplus(DIRS[d]), c), y), device_id_type=MESH,
            ).wait_recv()
            if h < HOPS and (d, f) in halves(h + 1):
                ag_copy(u, d, h + 1, f).start()

    def base_block(dy):
        block = lax.rem(y + dy, NY)
        width = 256

        def tile(n, carry):
            rows = pl.ds(pl.multiple_of(block * wv.shape[1] + n * width, width), width)
            cols = pl.ds(pl.multiple_of(n * width, width), width)
            base_s[dy, :, cols] = mm(gv[...], wv[rows, :], NT).astype(BF16)
            return carry

        lax.fori_loop(0, wv.shape[1] // width, tile, 0)

    def select(e, transposed):
        a, b = iota((ROWS, ROWS), 0), iota((ROWS, ROWS), 1)
        narrow, broad = (a, b) if transposed else (b, a)
        return jnp.where(narrow == e * RANK + (broad & (RANK - 1)), 1.0, 0.0).astype(BF16)

    toks_of = (tokx, tokg)
    project_of = (tokg, tokx)
    maps_of = (agb, aga)

    def project(u, first, count):
        def block(e, carry):
            wide_p = mm(project_of[u][e].reshape(ROWS, -1), maps_of[u][owner_z_of(e)], NT) * masks[e]
            part_low = mm(wide_p.astype(BF16), select(e, False))
            low_acc[...] = jnp.where(e == 0, part_low, low_acc[...] + part_low)
            return carry

        lax.fori_loop(first, first + count, block, 0)

    def low_sends(u):
        low_s[u] = low_acc[...].astype(BF16)
        for dy in (2, 1, 3):
            low_copy(u, dy).start()

    def spread(u):
        total = low_s[u].astype(F32)
        for dy in range(1, NY):
            low_copy(u, dy).wait_recv()
            total = total + low_r[u, dy - 1].astype(F32)
        low = total.astype(BF16)

        def block(e, carry):
            twice = mm(low, select(e, True)) * (2.0 * masks[e])
            if u == 0:
                wide[e] = twice.astype(BF16)
            wide_t[u, e] = twice.T.astype(BF16)
            return carry

        lax.fori_loop(0, NZ, block, 0)

    def lora(distance):
        e = (distance - 2) % NZ
        lora_s[e] = mm(wide[e], aga[zplus(distance)]).astype(BF16).reshape(PLANE, CAP, -1)

    def term(u, distance, f):
        e = (distance - 2) % NZ
        return mm(wide_t[u, e, f * HALF : (f + 1) * HALF, :], toks_of[u][e].reshape(ROWS, -1))

    def rs_target(d, h):
        return (HOPS + 1 - h) if d == 0 else -(HOPS + 1 - h)

    def rs_init(u):
        for h, part in ((1, FIRST), (2, SECOND)):
            for d, f in part:
                rs_s[u, d, h - 1, f] = term(u, rs_target(d, h), f).astype(BF16)
                rs_copy(u, d, h, f).start()

    def rs_step(u, h, part):
        for d, f in part:
            rs_copy(u, d, h, f).wait_recv()
            total = rs_r[u, d, h - 1, f].astype(F32) + term(u, rs_target(d, h + 1), f)
            rs_s[u, d, h, f] = total.astype(BF16)
            rs_copy(u, d, h + 1, f).start()

    def rs_last(u):
        out = (dgrad_ref, ugrad_ref)[u]
        own = [term(u, 0, f) for f in (0, 1)]
        for d, f in SECOND:
            rs_copy(u, d, HOPS, f).wait_recv()
            own[f] = own[f] + rs_r[u, d, HOPS - 1, f].astype(F32)
        for d, f in FIRST:
            rs_copy(u, d, HOPS, f).wait_recv()
            out[f * HALF : (f + 1) * HALF, :] = own[f] + rs_r[u, d, HOPS - 1, f].astype(F32)

    def finish(n, carry):
        rows = pl.ds(pl.multiple_of(n * ROWS, ROWS), ROWS)
        hot = jnp.where(iota((ROWS, PLANE * ROWS), 1) == idx_col[rows, :], 1.0, 0.0).astype(BF16)
        total = mm(hot, lora_r[...].reshape(PLANE * ROWS, -1)) + base_s[0, rows, :].astype(F32)
        for dy in range(1, NY):
            total = total + base_r[dy - 1, rows, :].astype(F32)
        dx_ref[rows, :] = total.astype(BF16)
        return carry

    def own_tokens(packed, landed):
        pack(gv if packed is gp else xv, packed, p)
        landed[:, pl.ds(p, 1)] = packed[pl.ds(p, 1)].reshape(NZ, 1, CAP, -1)

    every = range(len(PEERS))
    locals_["g"].wait()
    for i in every:
        xx, cc = column(PEERS[i])
        pack(gv, gp, xx * NC + cc)
        token_copy(0, i).start()
    forward(0, 1, FIRST)
    locals_["w"].wait()
    base_block(1)
    for f in (0, 1):
        base_copy(1, f).start()
    forward(0, 1, SECOND)
    base_block(3)
    for f in (0, 1):
        base_copy(3, f).start()
    forward(0, 2, FIRST)
    locals_["x"].wait()
    for i in every[:4]:
        xx, cc = column(PEERS[i])
        pack(xv, xp, xx * NC + cc)
        token_copy(1, i).start()
    forward(0, 2, SECOND)
    for i in every[4:]:
        xx, cc = column(PEERS[i])
        pack(xv, xp, xx * NC + cc)
        token_copy(1, i).start()
    for i in every:
        token_copy(2, i).start()
    forward(0, 3, FIRST)
    for d, f in FIRST:
        ag_copy(1, d, 1, f).start()
    own_tokens(gp, tokg)
    forward(0, 3, SECOND)
    for d, f in SECOND:
        ag_copy(1, d, 1, f).start()
    own_tokens(xp, tokx)
    for i in every:
        meta_copy(i).wait_recv()
    for e in range(NZ):
        masks[e] = jnp.broadcast_to(meta_r[:, e : e + 1, :], (PLANE, CAP, ROWS)).reshape(ROWS, ROWS)
    base_block(2)
    forward(0, HOPS, FIRST)
    locals_["b"].wait()
    forward(1, 1, FIRST)
    for i in every:
        token_copy(0, i).wait_recv()
    project(0, 0, NZ // 2)
    forward(1, 1, SECOND)
    project(0, NZ // 2, NZ // 2)
    low_sends(0)
    base_copy(2, 0).start()
    forward(1, 2, FIRST)
    spread(0)
    forward(1, 2, SECOND)
    locals_["a"].wait()
    for distance in (0, 1, -1, 2, -2):
        lora(distance)
    forward(1, 3, FIRST)
    for i in every:
        token_copy(1, i).wait_recv()
    forward(1, 3, SECOND)
    rs_init(0)
    lora(3)
    lora(-3)
    forward(1, HOPS, FIRST)
    lora(HOPS)
    for i in every:
        lora_copy(i).start()
    lora_r[pl.ds(p, 1)] = lora_s[:, pl.ds(p, 1)].reshape(1, NZ, CAP, -1)
    project(1, 0, NEAR)
    rs_step(0, 1, FIRST)
    for i in every:
        token_copy(2, i).wait_recv()
    rs_step(0, 2, SECOND)
    project(1, NEAR, NZ - NEAR)
    low_sends(1)
    base_copy(2, 1).start()
    rs_step(0, 2, FIRST)
    base_block(0)
    rs_step(0, 3, SECOND)
    spread(1)
    rs_step(0, 3, FIRST)
    rs_init(1)
    rs_last(0)
    rs_step(1, 1, FIRST)
    rs_step(1, 2, SECOND)
    rs_step(1, 2, FIRST)
    for i in every:
        lora_copy(i).wait_recv()
    for f in (0, 1):
        for dy in range(1, NY):
            base_copy(dy, f).wait_recv()
    lax.fori_loop(0, 2, finish, 0)
    rs_step(1, 3, SECOND)
    lax.fori_loop(2, 3, finish, 0)
    rs_step(1, 3, FIRST)
    lax.fori_loop(3, toks // ROWS, finish, 0)
    rs_last(1)

    for i in range(len(PEERS)):
        meta_copy(i).wait_send()
        for unit in range(3):
            token_copy(unit, i).wait_send()
        lora_copy(i).wait_send()
    for u in (0, 1):
        for h in range(1, HOPS + 1):
            for d, f in halves(h):
                ag_copy(u, d, h, f).wait_send()
            for f in (0, 1):
                for d in (0, 1):
                    if h > 1 or f == d:
                        rs_copy(u, d, h, f).wait_send()
        for dy in range(1, NY):
            low_copy(u, dy).wait_send()
    for dy in range(1, NY):
        for f in (0, 1):
            base_copy(dy, f).wait_send()


def _xzc(xc, z):
    return xc[0], z, xc[1]


def emit(*refs):
    copies = [pltpu.make_async_copy(refs[i], refs[3 + i], refs[6].at[i]) for i in range(3)]
    for copy in copies:
        copy.start()
    for copy in copies:
        copy.wait()


def on_device(
    activations,
    output_gradient,
    frozen_weight,
    adapter_down_weight,
    adapter_up_weight,
    adapter_slot_table,
    group_adapter_index,
    group_token_length,
):
    toks, feats = activations.shape
    own = adapter_down_weight.shape[0]
    any_spec = pl.BlockSpec(memory_space=pl.ANY)
    vmem_spec = pl.BlockSpec(memory_space=pltpu.VMEM)
    dma = pltpu.SemaphoreType.DMA
    n = len(PEERS)
    results = pl.pallas_call(
        kernel,
        out_shape=(
            pltpu.VMEM((toks, feats), BF16),
            pltpu.VMEM((own, feats), F32),
            pltpu.VMEM((own, feats), F32),
        ),
        in_specs=[any_spec] * 5 + [vmem_spec] * 3,
        out_specs=(vmem_spec,) * 3,
        scratch_shapes=[
            pltpu.VMEM((toks, feats), BF16),
            pltpu.VMEM((toks, feats), BF16),
            pltpu.VMEM(frozen_weight.shape, BF16),
            pltpu.VMEM((PLANE, NZ, CAP, feats), BF16),
            pltpu.VMEM((PLANE, NZ, CAP, feats), BF16),
            pltpu.VMEM((NZ, PLANE, CAP, feats), BF16),
            pltpu.VMEM((NZ, PLANE, CAP, feats), BF16),
            pltpu.VMEM((NZ, ROWS, feats), BF16),
            pltpu.VMEM((NZ, ROWS, feats), BF16),
            pltpu.VMEM((PLANE, NZ, ROWS), F32),
            pltpu.VMEM((PLANE, NZ, ROWS), F32),
            pltpu.VMEM((NZ, ROWS, ROWS), F32),
            pltpu.VMEM((ROWS, ROWS), F32),
            pltpu.VMEM((2, ROWS, ROWS), BF16),
            pltpu.VMEM((2, NY - 1, ROWS, ROWS), BF16),
            pltpu.VMEM((NZ, ROWS, ROWS), BF16),
            pltpu.VMEM((2, NZ, ROWS, ROWS), BF16),
            pltpu.VMEM((NY, toks, feats), BF16),
            pltpu.VMEM((NY - 1, toks, feats), BF16),
            pltpu.VMEM((NZ, PLANE, CAP, feats), BF16),
            pltpu.VMEM((PLANE, NZ, CAP, feats), BF16),
            pltpu.VMEM((2, 2, HOPS, 2, HALF, feats), BF16),
            pltpu.VMEM((2, 2, HOPS, 2, HALF, feats), BF16),
            pltpu.VMEM((1, toks), jnp.int32),
            pltpu.VMEM((toks, 1), jnp.int32),
            dma((5,)),
            dma((5, n)),
            dma((5, n)),
            dma((2, 2, HOPS, 2)),
            dma((2, 2, HOPS, 2)),
            dma((2, 2, HOPS, 2)),
            dma((2, 2, HOPS, 2)),
            dma((2, NY - 1)),
            dma((2, NY - 1)),
            dma((NY - 1, 2)),
            dma((NY - 1, 2)),
        ],
        compiler_params=pltpu.CompilerParams(
            collective_id=0, has_side_effects=True, vmem_limit_bytes=60 * 1024 * 1024
        ),
        name="lora_backward",
    )(
        activations,
        output_gradient,
        frozen_weight,
        adapter_down_weight,
        adapter_up_weight,
        adapter_slot_table.reshape(1, -1),
        group_adapter_index,
        group_token_length,
    )
    return pl.pallas_call(
        emit,
        out_shape=tuple(jax.ShapeDtypeStruct(r.shape, r.dtype) for r in results),
        in_specs=[vmem_spec] * 3,
        out_specs=(any_spec,) * 3,
        scratch_shapes=[dma((3,))],
        name="emit",
    )(*(pltpu.with_memory_space_constraint(r, pltpu.VMEM) for r in results))


def solution(mesh):
    in_specs = (
        P("adapter", "tensor"),
        P("adapter", "tensor"),
        P(None, "tensor"),
        P("adapter", "tensor"),
        P("adapter", "tensor"),
        P(),
        P("adapter", None),
        P("adapter", None),
    )
    out_specs = (P("adapter", "tensor"), P("adapter", "tensor"), P("adapter", "tensor"))
    return jax.shard_map(
        on_device, mesh=mesh, in_specs=in_specs, out_specs=out_specs, check_vma=False
    )
```

```python
import functools

import jax
import jax.numpy as jnp
from jax import lax
from jax.experimental import pallas as pl
from jax.experimental.pallas import tpu as pltpu
from jax.sharding import PartitionSpec as P

MESH = pl.DeviceIdType.MESH
F32 = jnp.float32
BF16 = jnp.bfloat16
RANK = 16
SLOTS = 8
NX, NZ, NC, NY = 4, 8, 2, 4
PLANE = NX * NC
CAP = 16
ROWS = PLANE * CAP
HALF = ROWS // 2
PEERS = ((2, 0), (2, 1), (1, 0), (1, 1), (3, 0), (3, 1), (0, 1))
DIRS = (1, NZ - 1)
FIRST, SECOND = ((0, 0), (1, 1)), ((0, 1), (1, 0))
NEAR = NZ // 2
HOPS = NZ // 2

NT = (((1,), (1,)), ((), ()))
NN = (((1,), (0,)), ((), ()))


def mm(a, b, dims=NN):
    return lax.dot_general(a, b, dims, preferred_element_type=F32)


def iota(shape, dim):
    return lax.broadcasted_iota(jnp.int32, shape, dim)


def kernel(
    x_hbm, g_hbm, w_hbm, ad_hbm, bu_hbm, table_ref, gai_ref, len_ref,
    dx_ref, dgrad_ref, ugrad_ref,
    xv, gv, wv, xp, gp, tokx, tokg, aga, agb, meta_s, meta_r, masks,
    low_acc, low_s, low_r, wide, wide_t, base_s, base_r, lora_s, lora_r, rs_s, rs_r, idx_row, idx_col,
    local_sem, x_send, x_recv, ag_send, ag_recv, rs_send, rs_recv, low_send, low_recv, base_send, base_recv,
):
    toks = gv.shape[0]
    me = lax.axis_index("adapter")
    y = lax.axis_index("tensor")
    x = lax.div(me, NZ * NC)
    z = lax.rem(lax.div(me, NC), NZ)
    c = lax.rem(me, NC)
    p = x * NC + c

    def at(xx, zz, cc):
        return (xx * NZ + zz) * NC + cc

    def zplus(d):
        return lax.rem(z + (d + 2 * NZ), NZ)

    def column(k):
        dx, dc = k
        return lax.rem(x + dx, NX), lax.rem(c + dc, NC)

    def owner_z_of(e):
        return zplus(e + 2)

    locals_ = {
        "g": pltpu.make_async_copy(g_hbm, gv, local_sem.at[0]),
        "x": pltpu.make_async_copy(x_hbm, xv, local_sem.at[1]),
        "b": pltpu.make_async_copy(bu_hbm, agb.at[z], local_sem.at[2]),
        "a": pltpu.make_async_copy(ad_hbm, aga.at[z], local_sem.at[3]),
        "w": pltpu.make_async_copy(w_hbm, wv, local_sem.at[4]),
    }

    def plane_copy(unit, i, src, dst):
        xx, cc = column(PEERS[i])
        return pltpu.make_async_remote_copy(
            src_ref=src, dst_ref=dst, send_sem=x_send.at[unit, i], recv_sem=x_recv.at[unit, i],
            device_id=(at(xx, z, cc), y), device_id_type=MESH,
        )

    def token_copy(unit, i):
        packed, landed, first, count = ((gp, tokg, 0, NZ), (xp, tokx, 0, NEAR), (xp, tokx, NEAR, NZ - NEAR))[unit]
        xx, cc = column(PEERS[i])
        entries = pl.ds(first, count)
        return plane_copy(unit, i, packed.at[xx * NC + cc, entries], landed.at[entries, p])

    def meta_copy(i):
        xx, cc = column(PEERS[i])
        return plane_copy(4, i, meta_s.at[xx * NC + cc], meta_r.at[p])

    def lora_copy(i):
        xx, cc = column(PEERS[i])
        return plane_copy(3, i, lora_s.at[:, xx * NC + cc], lora_r.at[p])

    def ag_copy(u, d, h, f):
        own = (bu_hbm, ad_hbm)[u]
        buf = (agb, aga)[u]
        rows = pl.ds(f * HALF, HALF)
        source = zplus(-(h - 1) if d == 0 else h - 1)
        src = own.at[rows] if h == 1 else buf.at[source, rows]
        return pltpu.make_async_remote_copy(
            src_ref=src, dst_ref=buf.at[source, rows],
            send_sem=ag_send.at[u, d, h - 1, f], recv_sem=ag_recv.at[u, d, h - 1, f],
            device_id=(at(x, zplus(DIRS[d]), c), y), device_id_type=MESH,
        )

    def rs_copy(u, d, h, f):
        return pltpu.make_async_remote_copy(
            src_ref=rs_s.at[u, d, h - 1, f], dst_ref=rs_r.at[u, d, h - 1, f],
            send_sem=rs_send.at[u, d, h - 1, f], recv_sem=rs_recv.at[u, d, h - 1, f],
            device_id=(at(x, zplus(DIRS[d]), c), y), device_id_type=MESH,
        )

    def low_copy(u, dy):
        return pltpu.make_async_remote_copy(
            src_ref=low_s.at[u], dst_ref=low_r.at[u, dy - 1],
            send_sem=low_send.at[u, dy - 1], recv_sem=low_recv.at[u, dy - 1],
            device_id=(me, lax.rem(y + dy, NY)), device_id_type=MESH,
        )

    def base_copy(dy, f):
        hop = dy if dy != 2 else (1, NY - 1)[f]
        rows = pl.ds(f * (toks // 2), toks // 2)
        return pltpu.make_async_remote_copy(
            src_ref=base_s.at[dy, rows], dst_ref=base_r.at[dy - 1, rows],
            send_sem=base_send.at[dy - 1, f], recv_sem=base_recv.at[dy - 1, f],
            device_id=(me, lax.rem(y + hop, NY)), device_id_type=MESH,
        )

    def halves(h):
        return FIRST + SECOND if h < HOPS else FIRST

    for name in ("g", "b", "x", "w", "a"):
        locals_[name].start()
    barrier = pltpu.get_barrier_semaphore()
    partners = [(at(*_xzc(column(k), z)), y) for k in PEERS]
    partners += [(at(x, zplus(d), c), y) for d in DIRS]
    partners += [(me, lax.rem(y + dy, NY)) for dy in range(1, NY)]
    for partner in partners:
        pl.semaphore_signal(barrier, inc=1, device_id=partner, device_id_type=MESH)

    ng = gai_ref.shape[1]
    eye = iota((ng, ng), 0) == iota((ng, ng), 1)

    def to_col(row):
        return jnp.sum(jnp.where(eye, row, 0.0), axis=1, keepdims=True)

    def to_row(col):
        return jnp.sum(jnp.where(eye, col, 0.0), axis=0, keepdims=True)

    gai_col = to_col(gai_ref[...].astype(F32)).astype(jnp.int32)
    len_row = len_ref[...].astype(F32)
    len_col = to_col(len_row)
    n_adapters = table_ref.shape[1]
    slot = jnp.sum(
        jnp.where(iota((ng, n_adapters), 1) == gai_col, table_ref[...].astype(F32), 0.0), axis=1, keepdims=True
    ).astype(jnp.int32)
    local = slot & (SLOTS - 1)
    owner_c = (slot >> 3) & 1
    owner_z = (slot >> 4) & (NZ - 1)
    owner_x = slot >> 7
    pair = (owner_x * NC + owner_c) * NZ + ((owner_z + (NZ - 2) + (NZ - z)) & (NZ - 1))
    start = jnp.sum(jnp.where(iota((ng, ng), 1) < iota((ng, ng), 0), len_row, 0.0), axis=1, keepdims=True)
    shift = (pair * CAP).astype(F32) - start
    end = start + len_col
    t_row = iota((ng, toks), 1).astype(F32)
    idx_row[...] = jnp.sum(
        jnp.where((t_row >= start) & (t_row < end), shift + t_row, 0.0), axis=0, keepdims=True
    ).astype(jnp.int32)
    t_col = iota((toks, ng), 0).astype(F32)
    idx_col[...] = jnp.sum(
        jnp.where((t_col >= to_row(start)) & (t_col < to_row(end)), to_row(shift) + t_col, 0.0), axis=1, keepdims=True
    ).astype(jnp.int32)
    pairs = PLANE * NZ
    slot_of_pair = jnp.sum(
        jnp.where(iota((pairs, ng), 0) == to_row(pair.astype(F32)).astype(jnp.int32), to_row(local.astype(F32)) + 1.0, 0.0),
        axis=1, keepdims=True,
    ).astype(jnp.int32)
    mask = jnp.where((iota((pairs, ROWS), 1) >> 4) + 1 == slot_of_pair, 1.0, 0.0)
    meta_s[...] = mask.reshape(PLANE, NZ, ROWS)
    meta_r[pl.ds(p, 1)] = meta_s[pl.ds(p, 1)]

    pl.semaphore_wait(barrier, len(partners))

    for d, f in halves(1):
        ag_copy(0, d, 1, f).start()
    for i in range(len(PEERS)):
        meta_copy(i).start()

    def pack(source, packed, q):
        hot = jnp.where(iota((ROWS, toks), 0) + q * ROWS == idx_row[...], 1.0, 0.0).astype(BF16)
        packed[q] = mm(hot, source[...]).astype(BF16).reshape(NZ, CAP, -1)

    def forward(u, h, part):
        for d, f in part:
            source = zplus(-h if d == 0 else h)
            buf = (agb, aga)[u]
            landed = buf.at[source, pl.ds(f * HALF, HALF)]
            pltpu.make_async_remote_copy(
                src_ref=landed, dst_ref=landed, send_sem=ag_send.at[u, d, h - 1, f],
                recv_sem=ag_recv.at[u, d, h - 1, f], device_id=(at(x, zplus(DIRS[d]), c), y), device_id_type=MESH,
            ).wait_recv()
            if h < HOPS and (d, f) in halves(h + 1):
                ag_copy(u, d, h + 1, f).start()

    def base_block(dy):
        block = lax.rem(y + dy, NY)
        width = 256

        def tile(n, carry):
            rows = pl.ds(pl.multiple_of(block * wv.shape[1] + n * width, width), width)
            cols = pl.ds(pl.multiple_of(n * width, width), width)
            base_s[dy, :, cols] = mm(gv[...], wv[rows, :], NT).astype(BF16)
            return carry

        lax.fori_loop(0, wv.shape[1] // width, tile, 0)

    def base_relay(dy, f):
        base_copy(2, f).wait_recv()
        rows = pl.ds(f * (toks // 2), toks // 2)
        base_s[dy, rows, :] = (base_s[dy, rows, :].astype(F32) + base_r[1, rows, :].astype(F32)).astype(BF16)
        base_copy(dy, f).start()

    def select(e, transposed):
        a, b = iota((ROWS, ROWS), 0), iota((ROWS, ROWS), 1)
        narrow, broad = (a, b) if transposed else (b, a)
        return jnp.where(narrow == e * RANK + (broad & (RANK - 1)), 1.0, 0.0).astype(BF16)

    toks_of = (tokx, tokg)
    project_of = (tokg, tokx)
    maps_of = (agb, aga)

    def project(u, first, count):
        def block(e, carry):
            wide_p = mm(project_of[u][e].reshape(ROWS, -1), maps_of[u][owner_z_of(e)], NT) * masks[e]
            part_low = mm(wide_p.astype(BF16), select(e, False))
            low_acc[...] = jnp.where(e == 0, part_low, low_acc[...] + part_low)
            return carry

        lax.fori_loop(first, first + count, block, 0)

    def low_sends(u):
        low_s[u] = low_acc[...].astype(BF16)
        for dy in (2, 1, 3):
            low_copy(u, dy).start()

    def spread(u):
        total = low_s[u].astype(F32)
        for dy in range(1, NY):
            low_copy(u, dy).wait_recv()
            total = total + low_r[u, dy - 1].astype(F32)
        low = total.astype(BF16)

        def block(e, carry):
            twice = mm(low, select(e, True)) * (2.0 * masks[e])
            if u == 0:
                wide[e] = twice.astype(BF16)
            wide_t[u, e] = twice.T.astype(BF16)
            return carry

        lax.fori_loop(0, NZ, block, 0)

    def lora(distance):
        e = (distance - 2) % NZ
        lora_s[e] = mm(wide[e], aga[zplus(distance)]).astype(BF16).reshape(PLANE, CAP, -1)

    def term(u, distance, f):
        e = (distance - 2) % NZ
        return mm(wide_t[u, e, f * HALF : (f + 1) * HALF, :], toks_of[u][e].reshape(ROWS, -1))

    def rs_target(d, h):
        return (HOPS + 1 - h) if d == 0 else -(HOPS + 1 - h)

    def rs_init(u):
        for h, part in ((1, FIRST), (2, SECOND)):
            for d, f in part:
                rs_s[u, d, h - 1, f] = term(u, rs_target(d, h), f).astype(BF16)
                rs_copy(u, d, h, f).start()

    def rs_step(u, h, part):
        for d, f in part:
            rs_copy(u, d, h, f).wait_recv()
            total = rs_r[u, d, h - 1, f].astype(F32) + term(u, rs_target(d, h + 1), f)
            rs_s[u, d, h, f] = total.astype(BF16)
            rs_copy(u, d, h + 1, f).start()

    def rs_last(u):
        out = (dgrad_ref, ugrad_ref)[u]
        own = [term(u, 0, f) for f in (0, 1)]
        for d, f in SECOND:
            rs_copy(u, d, HOPS, f).wait_recv()
            own[f] = own[f] + rs_r[u, d, HOPS - 1, f].astype(F32)
        for d, f in FIRST:
            rs_copy(u, d, HOPS, f).wait_recv()
            out[f * HALF : (f + 1) * HALF, :] = own[f] + rs_r[u, d, HOPS - 1, f].astype(F32)

    def finish(n, carry):
        rows = pl.ds(pl.multiple_of(n * ROWS, ROWS), ROWS)
        hot = jnp.where(iota((ROWS, PLANE * ROWS), 1) == idx_col[rows, :], 1.0, 0.0).astype(BF16)
        total = mm(hot, lora_r[...].reshape(PLANE * ROWS, -1)) + base_s[0, rows, :].astype(F32)
        for dy in (1, NY - 1):
            total = total + base_r[dy - 1, rows, :].astype(F32)
        dx_ref[rows, :] = total.astype(BF16)
        return carry

    def own_tokens(packed, landed):
        pack(gv if packed is gp else xv, packed, p)
        landed[:, pl.ds(p, 1)] = packed[pl.ds(p, 1)].reshape(NZ, 1, CAP, -1)

    every = range(len(PEERS))
    locals_["g"].wait()
    for i in every:
        xx, cc = column(PEERS[i])
        pack(gv, gp, xx * NC + cc)
        token_copy(0, i).start()
    forward(0, 1, FIRST)
    locals_["w"].wait()
    base_block(2)
    for f in (0, 1):
        base_copy(2, f).start()
    forward(0, 1, SECOND)
    base_block(1)
    base_copy(1, 1).start()
    forward(0, 2, FIRST)
    locals_["x"].wait()
    for i in every[:4]:
        xx, cc = column(PEERS[i])
        pack(xv, xp, xx * NC + cc)
        token_copy(1, i).start()
    forward(0, 2, SECOND)
    base_block(3)
    base_copy(3, 0).start()
    for i in every[4:]:
        xx, cc = column(PEERS[i])
        pack(xv, xp, xx * NC + cc)
        token_copy(1, i).start()
    for i in every:
        token_copy(2, i).start()
    forward(0, 3, FIRST)
    for d, f in FIRST:
        ag_copy(1, d, 1, f).start()
    own_tokens(gp, tokg)
    forward(0, 3, SECOND)
    for d, f in SECOND:
        ag_copy(1, d, 1, f).start()
    own_tokens(xp, tokx)
    for i in every:
        meta_copy(i).wait_recv()
    for e in range(NZ):
        masks[e] = jnp.broadcast_to(meta_r[:, e : e + 1, :], (PLANE, CAP, ROWS)).reshape(ROWS, ROWS)
    forward(0, HOPS, FIRST)
    locals_["b"].wait()
    forward(1, 1, FIRST)
    for i in every:
        token_copy(0, i).wait_recv()
    project(0, 0, NZ // 2)
    forward(1, 1, SECOND)
    project(0, NZ // 2, NZ // 2)
    low_sends(0)
    base_relay(1, 0)
    base_relay(3, 1)
    forward(1, 2, FIRST)
    spread(0)
    forward(1, 2, SECOND)
    locals_["a"].wait()
    for distance in (0, 1, -1, 2, -2):
        lora(distance)
    forward(1, 3, FIRST)
    for i in every:
        token_copy(1, i).wait_recv()
    forward(1, 3, SECOND)
    rs_init(0)
    lora(3)
    lora(-3)
    forward(1, HOPS, FIRST)
    lora(HOPS)
    for i in every:
        lora_copy(i).start()
    lora_r[pl.ds(p, 1)] = lora_s[:, pl.ds(p, 1)].reshape(1, NZ, CAP, -1)
    project(1, 0, NEAR)
    rs_step(0, 1, FIRST)
    for i in every:
        token_copy(2, i).wait_recv()
    rs_step(0, 2, SECOND)
    project(1, NEAR, NZ - NEAR)
    low_sends(1)
    rs_step(0, 2, FIRST)
    base_block(0)
    rs_step(0, 3, SECOND)
    spread(1)
    rs_step(0, 3, FIRST)
    rs_init(1)
    rs_last(0)
    rs_step(1, 1, FIRST)
    rs_step(1, 2, SECOND)
    rs_step(1, 2, FIRST)
    rs_step(1, 3, SECOND)
    rs_step(1, 3, FIRST)
    for i in every:
        lora_copy(i).wait_recv()
    for f in (0, 1):
        for dy in (1, NY - 1):
            base_copy(dy, f).wait_recv()
    lax.fori_loop(0, toks // ROWS, finish, 0)
    rs_last(1)

    for i in range(len(PEERS)):
        meta_copy(i).wait_send()
        for unit in range(3):
            token_copy(unit, i).wait_send()
        lora_copy(i).wait_send()
    for u in (0, 1):
        for h in range(1, HOPS + 1):
            for d, f in halves(h):
                ag_copy(u, d, h, f).wait_send()
            for f in (0, 1):
                for d in (0, 1):
                    if h > 1 or f == d:
                        rs_copy(u, d, h, f).wait_send()
        for dy in range(1, NY):
            low_copy(u, dy).wait_send()
    for dy in range(1, NY):
        for f in (0, 1):
            base_copy(dy, f).wait_send()


def _xzc(xc, z):
    return xc[0], z, xc[1]


def emit(*refs):
    copies = [pltpu.make_async_copy(refs[i], refs[3 + i], refs[6].at[i]) for i in range(3)]
    for copy in copies:
        copy.start()
    for copy in copies:
        copy.wait()


def on_device(
    activations,
    output_gradient,
    frozen_weight,
    adapter_down_weight,
    adapter_up_weight,
    adapter_slot_table,
    group_adapter_index,
    group_token_length,
):
    toks, feats = activations.shape
    own = adapter_down_weight.shape[0]
    any_spec = pl.BlockSpec(memory_space=pl.ANY)
    vmem_spec = pl.BlockSpec(memory_space=pltpu.VMEM)
    dma = pltpu.SemaphoreType.DMA
    n = len(PEERS)
    results = pl.pallas_call(
        kernel,
        out_shape=(
            pltpu.VMEM((toks, feats), BF16),
            pltpu.VMEM((own, feats), F32),
            pltpu.VMEM((own, feats), F32),
        ),
        in_specs=[any_spec] * 5 + [vmem_spec] * 3,
        out_specs=(vmem_spec,) * 3,
        scratch_shapes=[
            pltpu.VMEM((toks, feats), BF16),
            pltpu.VMEM((toks, feats), BF16),
            pltpu.VMEM(frozen_weight.shape, BF16),
            pltpu.VMEM((PLANE, NZ, CAP, feats), BF16),
            pltpu.VMEM((PLANE, NZ, CAP, feats), BF16),
            pltpu.VMEM((NZ, PLANE, CAP, feats), BF16),
            pltpu.VMEM((NZ, PLANE, CAP, feats), BF16),
            pltpu.VMEM((NZ, ROWS, feats), BF16),
            pltpu.VMEM((NZ, ROWS, feats), BF16),
            pltpu.VMEM((PLANE, NZ, ROWS), F32),
            pltpu.VMEM((PLANE, NZ, ROWS), F32),
            pltpu.VMEM((NZ, ROWS, ROWS), F32),
            pltpu.VMEM((ROWS, ROWS), F32),
            pltpu.VMEM((2, ROWS, ROWS), BF16),
            pltpu.VMEM((2, NY - 1, ROWS, ROWS), BF16),
            pltpu.VMEM((NZ, ROWS, ROWS), BF16),
            pltpu.VMEM((2, NZ, ROWS, ROWS), BF16),
            pltpu.VMEM((NY, toks, feats), BF16),
            pltpu.VMEM((NY - 1, toks, feats), BF16),
            pltpu.VMEM((NZ, PLANE, CAP, feats), BF16),
            pltpu.VMEM((PLANE, NZ, CAP, feats), BF16),
            pltpu.VMEM((2, 2, HOPS, 2, HALF, feats), BF16),
            pltpu.VMEM((2, 2, HOPS, 2, HALF, feats), BF16),
            pltpu.VMEM((1, toks), jnp.int32),
            pltpu.VMEM((toks, 1), jnp.int32),
            dma((5,)),
            dma((5, n)),
            dma((5, n)),
            dma((2, 2, HOPS, 2)),
            dma((2, 2, HOPS, 2)),
            dma((2, 2, HOPS, 2)),
            dma((2, 2, HOPS, 2)),
            dma((2, NY - 1)),
            dma((2, NY - 1)),
            dma((NY - 1, 2)),
            dma((NY - 1, 2)),
        ],
        compiler_params=pltpu.CompilerParams(
            collective_id=0, has_side_effects=True, vmem_limit_bytes=60 * 1024 * 1024
        ),
        name="lora_backward",
    )(
        activations,
        output_gradient,
        frozen_weight,
        adapter_down_weight,
        adapter_up_weight,
        adapter_slot_table.reshape(1, -1),
        group_adapter_index,
        group_token_length,
    )
    return pl.pallas_call(
        emit,
        out_shape=tuple(jax.ShapeDtypeStruct(r.shape, r.dtype) for r in results),
        in_specs=[vmem_spec] * 3,
        out_specs=(any_spec,) * 3,
        scratch_shapes=[dma((3,))],
        name="emit",
    )(*(pltpu.with_memory_space_constraint(r, pltpu.VMEM) for r in results))


def solution(mesh):
    in_specs = (
        P("adapter", "tensor"),
        P("adapter", "tensor"),
        P(None, "tensor"),
        P("adapter", "tensor"),
        P("adapter", "tensor"),
        P(),
        P("adapter", None),
        P("adapter", None),
    )
    out_specs = (P("adapter", "tensor"), P("adapter", "tensor"), P("adapter", "tensor"))
    return jax.shard_map(
        on_device, mesh=mesh, in_specs=in_specs, out_specs=out_specs, check_vma=False
    )
```

```python
import functools

import jax
import jax.numpy as jnp
from jax import lax
from jax.experimental import pallas as pl
from jax.experimental.pallas import tpu as pltpu
from jax.sharding import PartitionSpec as P

MESH = pl.DeviceIdType.MESH
F32 = jnp.float32
BF16 = jnp.bfloat16
RANK = 16
SLOTS = 8
NX, NZ, NC, NY = 4, 8, 2, 4
PLANE = NX * NC
CAP = 16
ROWS = PLANE * CAP
HALF = ROWS // 2
PEERS = ((2, 0), (2, 1), (1, 0), (1, 1), (3, 0), (3, 1), (0, 1))
DIRS = (1, NZ - 1)
FIRST, SECOND = ((0, 0), (1, 1)), ((0, 1), (1, 0))
HOPS = NZ // 2
PIECES = 2
TOKENS = ((0, 0, 3), (1, 0, 3), (0, 3, 2), (1, 3, 2), (0, 5, 3), (1, 5, 2), (1, 7, 1))
LOWS = (((0, 3), (3, 2), (5, 3)), ((0, 5), (5, 3)))

NT = (((1,), (1,)), ((), ()))
NN = (((1,), (0,)), ((), ()))


def mm(a, b, dims=NN):
    return lax.dot_general(a, b, dims, preferred_element_type=F32)


def iota(shape, dim):
    return lax.broadcasted_iota(jnp.int32, shape, dim)


def entry_of(distance):
    ahead = distance % NZ
    return max(NZ - 1 - 2 * min(ahead, NZ - ahead) + (ahead > HOPS), 0)


def kernel(
    x_hbm, g_hbm, w_hbm, ad_hbm, bu_hbm, table_hbm, gai_hbm, len_hbm,
    dx_ref, dgrad_ref, ugrad_ref,
    xv, gv, wv, xp, gp, tokx, tokg, aga, agb, meta_s, meta_r, masks,
    low_acc, low_s, low_r, wide, wide_t, base_s, base_r, lora_s, lora_r, rs_s, rs_r, idx_row, idx_col, table_ref, gai_ref, len_ref,
    local_sem, x_send, x_recv, ag_send, ag_recv, rs_send, rs_recv, low_send, low_recv, base_send, base_recv,
):
    toks = gv.shape[0]
    me = lax.axis_index("adapter")
    y = lax.axis_index("tensor")
    x = lax.div(me, NZ * NC)
    z = lax.rem(lax.div(me, NC), NZ)
    c = lax.rem(me, NC)
    p = x * NC + c

    def at(xx, zz, cc):
        return (xx * NZ + zz) * NC + cc

    def zplus(d):
        return lax.rem(z + (d + 2 * NZ), NZ)

    def column(k):
        dx, dc = k
        return lax.rem(x + dx, NX), lax.rem(c + dc, NC)

    def owner_z_of(e):
        distance, odd = lax.div(NZ - e, 2), lax.rem(e, 2)
        return zplus(odd * distance + (1 - odd) * (NZ - distance))

    locals_ = {
        "g": pltpu.make_async_copy(g_hbm, gv, local_sem.at[0]),
        "x": pltpu.make_async_copy(x_hbm, xv, local_sem.at[1]),
        "b": pltpu.make_async_copy(bu_hbm, agb.at[z], local_sem.at[2]),
        "a": pltpu.make_async_copy(ad_hbm, aga.at[z], local_sem.at[3]),
        "w": pltpu.make_async_copy(w_hbm, wv, local_sem.at[4]),
        "table": pltpu.make_async_copy(table_hbm, table_ref, local_sem.at[5]),
        "gai": pltpu.make_async_copy(gai_hbm, gai_ref, local_sem.at[6]),
        "len": pltpu.make_async_copy(len_hbm, len_ref, local_sem.at[7]),
    }

    def plane_copy(unit, i, src, dst):
        xx, cc = column(PEERS[i])
        return pltpu.make_async_remote_copy(
            src_ref=src, dst_ref=dst, send_sem=x_send.at[unit, i], recv_sem=x_recv.at[unit, i],
            device_id=(at(xx, z, cc), y), device_id_type=MESH,
        )

    def token_copy(unit, i):
        kind, first, count = TOKENS[unit]
        packed, landed = ((gp, tokg), (xp, tokx))[kind]
        xx, cc = column(PEERS[i])
        entries = pl.ds(first, count)
        return plane_copy(unit, i, packed.at[xx * NC + cc, entries], landed.at[entries, p])

    def meta_copy(i):
        xx, cc = column(PEERS[i])
        return plane_copy(len(TOKENS) + 1, i, meta_s.at[xx * NC + cc], meta_r.at[p])

    def lora_copy(i):
        xx, cc = column(PEERS[i])
        return plane_copy(len(TOKENS), i, lora_s.at[:, xx * NC + cc], lora_r.at[p])

    def ag_copy(u, d, h, f):
        own = (bu_hbm, ad_hbm)[u]
        buf = (agb, aga)[u]
        rows = pl.ds(f * HALF, HALF)
        source = zplus(-(h - 1) if d == 0 else h - 1)
        src = own.at[rows] if h == 1 else buf.at[source, rows]
        return pltpu.make_async_remote_copy(
            src_ref=src, dst_ref=buf.at[source, rows],
            send_sem=ag_send.at[u, d, h - 1, f], recv_sem=ag_recv.at[u, d, h - 1, f],
            device_id=(at(x, zplus(DIRS[d]), c), y), device_id_type=MESH,
        )

    def rs_copy(u, d, h, f):
        return pltpu.make_async_remote_copy(
            src_ref=rs_s.at[u, d, h - 1, f], dst_ref=rs_r.at[u, d, h - 1, f],
            send_sem=rs_send.at[u, d, h - 1, f], recv_sem=rs_recv.at[u, d, h - 1, f],
            device_id=(at(x, zplus(DIRS[d]), c), y), device_id_type=MESH,
        )

    def low_copy(u, part, dy):
        return pltpu.make_async_remote_copy(
            src_ref=low_s.at[u, part], dst_ref=low_r.at[u, part, dy - 1],
            send_sem=low_send.at[u, part, dy - 1], recv_sem=low_recv.at[u, part, dy - 1],
            device_id=(me, lax.rem(y + dy, NY)), device_id_type=MESH,
        )

    def base_copy(dy, f):
        hop = dy if dy != 2 else (1, NY - 1)[f]
        rows = pl.ds(f * (toks // PIECES), toks // PIECES)
        return pltpu.make_async_remote_copy(
            src_ref=base_s.at[dy, rows], dst_ref=base_r.at[dy - 1, rows],
            send_sem=base_send.at[dy - 1, f], recv_sem=base_recv.at[dy - 1, f],
            device_id=(me, lax.rem(y + hop, NY)), device_id_type=MESH,
        )

    def halves(h):
        return FIRST + SECOND if h < HOPS else FIRST

    barrier = pltpu.get_barrier_semaphore()
    partners = [(at(*_xzc(column(k), z)), y) for k in PEERS]
    partners += [(at(x, zplus(d), c), y) for d in DIRS]
    partners += [(me, lax.rem(y + dy, NY)) for dy in range(1, NY)]
    for partner in partners:
        pl.semaphore_signal(barrier, inc=1, device_id=partner, device_id_type=MESH)
    small = ("table", "gai", "len")
    for name in small + ("g", "x", "w", "b", "a"):
        locals_[name].start()
    for name in small:
        locals_[name].wait()

    ng = gai_ref.shape[1]
    eye = iota((ng, ng), 0) == iota((ng, ng), 1)

    def to_col(row):
        return jnp.sum(jnp.where(eye, row, 0.0), axis=1, keepdims=True)

    def to_row(col):
        return jnp.sum(jnp.where(eye, col, 0.0), axis=0, keepdims=True)

    gai_col = to_col(gai_ref[...].astype(F32)).astype(jnp.int32)
    len_row = len_ref[...].astype(F32)
    len_col = to_col(len_row)
    n_adapters = table_ref.shape[1]
    slot = jnp.sum(
        jnp.where(iota((ng, n_adapters), 1) == gai_col, table_ref[...].astype(F32), 0.0), axis=1, keepdims=True
    ).astype(jnp.int32)
    local = slot & (SLOTS - 1)
    owner_c = (slot >> 3) & 1
    owner_z = (slot >> 4) & (NZ - 1)
    owner_x = slot >> 7
    ahead = (owner_z + (NZ - z)) & (NZ - 1)
    entry = jnp.maximum(NZ - 1 - 2 * jnp.minimum(ahead, NZ - ahead) + jnp.where(ahead > HOPS, 1, 0), 0)
    pair = (owner_x * NC + owner_c) * NZ + entry
    start = jnp.sum(jnp.where(iota((ng, ng), 1) < iota((ng, ng), 0), len_row, 0.0), axis=1, keepdims=True)
    shift = (pair * CAP).astype(F32) - start
    end = start + len_col
    t_row = iota((ng, toks), 1).astype(F32)
    idx_row[...] = jnp.sum(
        jnp.where((t_row >= start) & (t_row < end), shift + t_row, 0.0), axis=0, keepdims=True
    ).astype(jnp.int32)
    t_col = iota((toks, ng), 0).astype(F32)
    idx_col[...] = jnp.sum(
        jnp.where((t_col >= to_row(start)) & (t_col < to_row(end)), to_row(shift) + t_col, 0.0), axis=1, keepdims=True
    ).astype(jnp.int32)
    pairs = PLANE * NZ
    slot_of_pair = jnp.sum(
        jnp.where(iota((pairs, ng), 0) == to_row(pair.astype(F32)).astype(jnp.int32), to_row(local.astype(F32)) + 1.0, 0.0),
        axis=1, keepdims=True,
    ).astype(jnp.int32)
    mask = jnp.where((iota((pairs, ROWS), 1) >> 4) + 1 == slot_of_pair, 1.0, 0.0)
    meta_s[...] = mask.reshape(PLANE, NZ, ROWS)
    meta_r[pl.ds(p, 1)] = meta_s[pl.ds(p, 1)]

    pl.semaphore_wait(barrier, len(partners))

    for d, f in halves(1):
        ag_copy(0, d, 1, f).start()

    for i in range(len(PEERS)):
        meta_copy(i).start()

    def pack(source, packed, q):
        hot = jnp.where(iota((ROWS, toks), 0) + q * ROWS == idx_row[...], 1.0, 0.0).astype(BF16)
        packed[q] = mm(hot, source[...]).astype(BF16).reshape(NZ, CAP, -1)

    def forward(u, h, part):
        for d, f in part:
            source = zplus(-h if d == 0 else h)
            buf = (agb, aga)[u]
            landed = buf.at[source, pl.ds(f * HALF, HALF)]
            pltpu.make_async_remote_copy(
                src_ref=landed, dst_ref=landed, send_sem=ag_send.at[u, d, h - 1, f],
                recv_sem=ag_recv.at[u, d, h - 1, f], device_id=(at(x, zplus(DIRS[d]), c), y), device_id_type=MESH,
            ).wait_recv()
            if h < HOPS and (d, f) in halves(h + 1):
                ag_copy(u, d, h + 1, f).start()

    def base_block(dy):
        block = lax.rem(y + dy, NY)
        width = 256

        def tile(n, carry):
            rows = pl.ds(pl.multiple_of(block * wv.shape[1] + n * width, width), width)
            cols = pl.ds(pl.multiple_of(n * width, width), width)
            base_s[dy, :, cols] = mm(gv[...], wv[rows, :], NT).astype(BF16)
            return carry

        lax.fori_loop(0, wv.shape[1] // width, tile, 0)

    def base_relay(dy, f):
        base_copy(2, f).wait_recv()
        rows = pl.ds(f * (toks // PIECES), toks // PIECES)
        base_s[dy, rows, :] = (base_s[dy, rows, :].astype(F32) + base_r[1, rows, :].astype(F32)).astype(BF16)
        base_copy(dy, f).start()

    def select(e, transposed):
        a, b = iota((ROWS, ROWS), 0), iota((ROWS, ROWS), 1)
        narrow, broad = (a, b) if transposed else (b, a)
        return jnp.where(narrow == e * RANK + (broad & (RANK - 1)), 1.0, 0.0).astype(BF16)

    toks_of = (tokx, tokg)
    project_of = (tokg, tokx)
    maps_of = (agb, aga)

    def project(u, part):
        first, count = LOWS[u][part]

        def block(e, carry):
            wide_p = mm(project_of[u][e].reshape(ROWS, -1), maps_of[u][owner_z_of(e)], NT) * masks[e]
            part_low = mm(wide_p.astype(BF16), select(e, False))
            low_acc[...] = jnp.where(e == first, part_low, low_acc[...] + part_low)
            return carry

        lax.fori_loop(first, first + count, block, 0)
        low_s[u, part] = low_acc[...].astype(BF16)
        for dy in (2, 1, 3):
            low_copy(u, part, dy).start()

    def spread(u, part):
        total = low_s[u, part].astype(F32)
        for dy in range(1, NY):
            low_copy(u, part, dy).wait_recv()
            total = total + low_r[u, part, dy - 1].astype(F32)
        low = total.astype(BF16)
        first, count = LOWS[u][part]

        def block(e, carry):
            twice = mm(low, select(e, True)) * (2.0 * masks[e])
            if u == 0:
                wide[e] = twice.astype(BF16)
            wide_t[u, e] = twice.T.astype(BF16)
            return carry

        lax.fori_loop(first, first + count, block, 0)

    def lora(distance):
        e = entry_of(distance)
        lora_s[e] = mm(wide[e], aga[zplus(distance)]).astype(BF16).reshape(PLANE, CAP, -1)

    def term(u, distance, f):
        e = entry_of(distance)
        return mm(wide_t[u, e, f * HALF : (f + 1) * HALF, :], toks_of[u][e].reshape(ROWS, -1))

    def rs_target(d, h):
        return (HOPS + 1 - h) if d == 0 else -(HOPS + 1 - h)

    def rs_init(u):
        for h, part in ((1, FIRST), (2, SECOND)):
            for d, f in part:
                rs_s[u, d, h - 1, f] = term(u, rs_target(d, h), f).astype(BF16)
                rs_copy(u, d, h, f).start()

    def rs_step(u, h, part):
        for d, f in part:
            rs_copy(u, d, h, f).wait_recv()
            total = rs_r[u, d, h - 1, f].astype(F32) + term(u, rs_target(d, h + 1), f)
            rs_s[u, d, h, f] = total.astype(BF16)
            rs_copy(u, d, h + 1, f).start()

    def rs_last(u):
        out = (dgrad_ref, ugrad_ref)[u]
        own = [term(u, 0, f) for f in (0, 1)]
        for d, f in SECOND:
            rs_copy(u, d, HOPS, f).wait_recv()
            own[f] = own[f] + rs_r[u, d, HOPS - 1, f].astype(F32)
        for d, f in FIRST:
            rs_copy(u, d, HOPS, f).wait_recv()
            out[f * HALF : (f + 1) * HALF, :] = own[f] + rs_r[u, d, HOPS - 1, f].astype(F32)

    def finish(n, carry):
        rows = pl.ds(pl.multiple_of(n * ROWS, ROWS), ROWS)
        hot = jnp.where(iota((ROWS, PLANE * ROWS), 1) == idx_col[rows, :], 1.0, 0.0).astype(BF16)
        total = mm(hot, lora_r[...].reshape(PLANE * ROWS, -1)) + base_s[0, rows, :].astype(F32)
        for dy in (1, NY - 1):
            total = total + base_r[dy - 1, rows, :].astype(F32)
        dx_ref[rows, :] = total.astype(BF16)
        return carry

    def own_tokens(packed, landed):
        pack(gv if packed is gp else xv, packed, p)
        landed[:, pl.ds(p, 1)] = packed[pl.ds(p, 1)].reshape(NZ, 1, CAP, -1)

    every = range(len(PEERS))
    locals_["g"].wait()
    for i in every:
        xx, cc = column(PEERS[i])
        pack(gv, gp, xx * NC + cc)
        token_copy(0, i).start()
    forward(0, 1, FIRST)
    locals_["w"].wait()
    base_block(2)
    for f in (0, 1):
        base_copy(2, f).start()
    forward(0, 1, SECOND)
    base_block(1)
    base_copy(1, 1).start()
    forward(0, 2, FIRST)
    locals_["x"].wait()
    for i in every[:4]:
        xx, cc = column(PEERS[i])
        pack(xv, xp, xx * NC + cc)
        token_copy(1, i).start()
    forward(0, 2, SECOND)
    base_block(3)
    base_copy(3, 0).start()
    for i in every[4:]:
        xx, cc = column(PEERS[i])
        pack(xv, xp, xx * NC + cc)
        token_copy(1, i).start()
    for unit in range(2, len(TOKENS)):
        for i in every:
            token_copy(unit, i).start()
    forward(0, 3, FIRST)
    for d, f in FIRST:
        ag_copy(1, d, 1, f).start()
    own_tokens(gp, tokg)
    for i in every:
        meta_copy(i).wait_recv()
    for e in range(NZ):
        masks[e] = jnp.broadcast_to(meta_r[:, e : e + 1, :], (PLANE, CAP, ROWS)).reshape(ROWS, ROWS)
    forward(0, 3, SECOND)
    for d, f in SECOND:
        ag_copy(1, d, 1, f).start()
    own_tokens(xp, tokx)
    forward(0, HOPS, FIRST)
    locals_["b"].wait()

    def landed(unit):
        for i in every:
            token_copy(unit, i).wait_recv()

    landed(0)
    project(0, 0)
    forward(1, 1, FIRST)
    forward(1, 1, SECOND)
    base_block(0)
    forward(1, 2, FIRST)
    landed(2)
    project(0, 1)
    base_relay(1, 0)
    base_relay(3, 1)
    locals_["a"].wait()
    forward(1, 2, SECOND)
    forward(1, 3, FIRST)
    forward(1, 3, SECOND)
    spread(0, 0)
    landed(1)
    rs_init(0)
    lora(3)
    lora(-3)
    forward(1, HOPS, FIRST)
    lora(HOPS)
    spread(0, 1)
    lora(2)
    lora(-2)
    rs_step(0, 1, FIRST)
    landed(3)
    project(1, 0)
    landed(4)
    project(0, 2)
    rs_step(0, 2, SECOND)
    rs_step(0, 2, FIRST)
    spread(0, 2)
    for distance in (0, 1, -1):
        lora(distance)
    for i in every:
        lora_copy(i).start()
    lora_r[pl.ds(p, 1)] = lora_s[:, pl.ds(p, 1)].reshape(1, NZ, CAP, -1)
    landed(5)
    rs_step(0, 3, SECOND)
    landed(6)
    project(1, 1)
    rs_step(0, 3, FIRST)
    spread(1, 0)
    rs_init(1)
    rs_last(0)
    spread(1, 1)
    rs_step(1, 1, FIRST)
    rs_step(1, 2, SECOND)
    rs_step(1, 2, FIRST)
    rs_step(1, 3, SECOND)
    rs_step(1, 3, FIRST)
    for i in every:
        lora_copy(i).wait_recv()
    for f in range(PIECES):
        for dy in (1, NY - 1):
            base_copy(dy, f).wait_recv()
    lax.fori_loop(0, toks // ROWS, finish, 0)
    rs_last(1)

    for i in range(len(PEERS)):
        meta_copy(i).wait_send()
        for unit in range(len(TOKENS)):
            token_copy(unit, i).wait_send()
        lora_copy(i).wait_send()
    for u in (0, 1):
        for h in range(1, HOPS + 1):
            for d, f in halves(h):
                ag_copy(u, d, h, f).wait_send()
            for f in (0, 1):
                for d in (0, 1):
                    if h > 1 or f == d:
                        rs_copy(u, d, h, f).wait_send()
        for dy in range(1, NY):
            for part in range(len(LOWS[u])):
                low_copy(u, part, dy).wait_send()
    for dy in range(1, NY):
        for f in range(PIECES):
            base_copy(dy, f).wait_send()


def _xzc(xc, z):
    return xc[0], z, xc[1]


def emit(*refs):
    copies = [pltpu.make_async_copy(refs[i], refs[3 + i], refs[6].at[i]) for i in range(3)]
    for copy in copies:
        copy.start()
    for copy in copies:
        copy.wait()


def on_device(
    activations,
    output_gradient,
    frozen_weight,
    adapter_down_weight,
    adapter_up_weight,
    adapter_slot_table,
    group_adapter_index,
    group_token_length,
):
    toks, feats = activations.shape
    own = adapter_down_weight.shape[0]
    any_spec = pl.BlockSpec(memory_space=pl.ANY)
    vmem_spec = pl.BlockSpec(memory_space=pltpu.VMEM)
    dma = pltpu.SemaphoreType.DMA
    n = len(PEERS)
    results = pl.pallas_call(
        kernel,
        out_shape=(
            pltpu.VMEM((toks, feats), BF16),
            pltpu.VMEM((own, feats), F32),
            pltpu.VMEM((own, feats), F32),
        ),
        in_specs=[any_spec] * 8,
        out_specs=(vmem_spec,) * 3,
        scratch_shapes=[
            pltpu.VMEM((toks, feats), BF16),
            pltpu.VMEM((toks, feats), BF16),
            pltpu.VMEM(frozen_weight.shape, BF16),
            pltpu.VMEM((PLANE, NZ, CAP, feats), BF16),
            pltpu.VMEM((PLANE, NZ, CAP, feats), BF16),
            pltpu.VMEM((NZ, PLANE, CAP, feats), BF16),
            pltpu.VMEM((NZ, PLANE, CAP, feats), BF16),
            pltpu.VMEM((NZ, ROWS, feats), BF16),
            pltpu.VMEM((NZ, ROWS, feats), BF16),
            pltpu.VMEM((PLANE, NZ, ROWS), F32),
            pltpu.VMEM((PLANE, NZ, ROWS), F32),
            pltpu.VMEM((NZ, ROWS, ROWS), F32),
            pltpu.VMEM((ROWS, ROWS), F32),
            pltpu.VMEM((2, 3, ROWS, ROWS), BF16),
            pltpu.VMEM((2, 3, NY - 1, ROWS, ROWS), BF16),
            pltpu.VMEM((NZ, ROWS, ROWS), BF16),
            pltpu.VMEM((2, NZ, ROWS, ROWS), BF16),
            pltpu.VMEM((NY, toks, feats), BF16),
            pltpu.VMEM((NY - 1, toks, feats), BF16),
            pltpu.VMEM((NZ, PLANE, CAP, feats), BF16),
            pltpu.VMEM((PLANE, NZ, CAP, feats), BF16),
            pltpu.VMEM((2, 2, HOPS, 2, HALF, feats), BF16),
            pltpu.VMEM((2, 2, HOPS, 2, HALF, feats), BF16),
            pltpu.VMEM((1, toks), jnp.int32),
            pltpu.VMEM((toks, 1), jnp.int32),
            pltpu.VMEM((1, adapter_slot_table.shape[0]), jnp.int32),
            pltpu.VMEM(group_adapter_index.shape, jnp.int32),
            pltpu.VMEM(group_token_length.shape, jnp.int32),
            dma((8,)),
            dma((len(TOKENS) + 2, n)),
            dma((len(TOKENS) + 2, n)),
            dma((2, 2, HOPS, 2)),
            dma((2, 2, HOPS, 2)),
            dma((2, 2, HOPS, 2)),
            dma((2, 2, HOPS, 2)),
            dma((2, 3, NY - 1)),
            dma((2, 3, NY - 1)),
            dma((NY - 1, PIECES)),
            dma((NY - 1, PIECES)),
        ],
        compiler_params=pltpu.CompilerParams(
            collective_id=0, has_side_effects=True, vmem_limit_bytes=60 * 1024 * 1024
        ),
        name="lora_backward",
    )(
        activations,
        output_gradient,
        frozen_weight,
        adapter_down_weight,
        adapter_up_weight,
        adapter_slot_table.reshape(1, -1),
        group_adapter_index,
        group_token_length,
    )
    return pl.pallas_call(
        emit,
        out_shape=tuple(jax.ShapeDtypeStruct(r.shape, r.dtype) for r in results),
        in_specs=[vmem_spec] * 3,
        out_specs=(any_spec,) * 3,
        scratch_shapes=[dma((3,))],
        name="emit",
    )(*(pltpu.with_memory_space_constraint(r, pltpu.VMEM) for r in results))


def solution(mesh):
    in_specs = (
        P("adapter", "tensor"),
        P("adapter", "tensor"),
        P(None, "tensor"),
        P("adapter", "tensor"),
        P("adapter", "tensor"),
        P(),
        P("adapter", None),
        P("adapter", None),
    )
    out_specs = (P("adapter", "tensor"), P("adapter", "tensor"), P("adapter", "tensor"))
    return jax.shard_map(
        on_device, mesh=mesh, in_specs=in_specs, out_specs=out_specs, check_vma=False
    )
```

```python
import functools

import jax
import jax.numpy as jnp
from jax import lax
from jax.experimental import pallas as pl
from jax.experimental.pallas import tpu as pltpu
from jax.sharding import PartitionSpec as P

MESH = pl.DeviceIdType.MESH
F32 = jnp.float32
BF16 = jnp.bfloat16
RANK = 16
SLOTS = 8
NX, NZ, NC, NY = 4, 8, 2, 4
PLANE = NX * NC
CAP = 16
ROWS = PLANE * CAP
HALF = ROWS // 2
PEERS = ((1, 0), (3, 0), (1, 1), (3, 1), (2, 0), (2, 1), (0, 1))
DIRS = (1, NZ - 1)
FIRST, SECOND = ((0, 0), (1, 1)), ((0, 1), (1, 0))
HOPS = NZ // 2
PIECES = 2
TOKENS = ((0, 0, 3), (1, 0, 3), (0, 3, 2), (1, 3, 2), (0, 5, 3), (1, 5, 2), (1, 7, 1))
LOWS = (((0, 3), (3, 2), (5, 3)), ((0, 5), (5, 3)))

NT = (((1,), (1,)), ((), ()))
NN = (((1,), (0,)), ((), ()))


def mm(a, b, dims=NN):
    return lax.dot_general(a, b, dims, preferred_element_type=F32)


def iota(shape, dim):
    return lax.broadcasted_iota(jnp.int32, shape, dim)


def entry_of(distance):
    ahead = distance % NZ
    return max(NZ - 1 - 2 * min(ahead, NZ - ahead) + (ahead > HOPS), 0)


def kernel(
    x_hbm, g_hbm, w_hbm, ad_hbm, bu_hbm, table_hbm, gai_hbm, len_hbm,
    dx_ref, dgrad_ref, ugrad_ref,
    xv, gv, wv, xp, gp, tokx, tokg, aga, agb, meta_s, meta_r, masks,
    low_acc, low_s, low_r, wide, wide_t, base_s, base_r, lora_s, lora_r, rs_s, rs_r, idx_row, idx_col, table_ref, gai_ref, len_ref,
    local_sem, x_send, x_recv, ag_send, ag_recv, rs_send, rs_recv, low_send, low_recv, base_send, base_recv,
):
    toks = gv.shape[0]
    me = lax.axis_index("adapter")
    y = lax.axis_index("tensor")
    x = lax.div(me, NZ * NC)
    z = lax.rem(lax.div(me, NC), NZ)
    c = lax.rem(me, NC)
    p = x * NC + c

    def at(xx, zz, cc):
        return (xx * NZ + zz) * NC + cc

    def zplus(d):
        return lax.rem(z + (d + 2 * NZ), NZ)

    def column(k):
        dx, dc = k
        return lax.rem(x + dx, NX), lax.rem(c + dc, NC)

    def owner_z_of(e):
        distance, odd = lax.div(NZ - e, 2), lax.rem(e, 2)
        return zplus(odd * distance + (1 - odd) * (NZ - distance))

    locals_ = {
        "g": pltpu.make_async_copy(g_hbm, gv, local_sem.at[0]),
        "x": pltpu.make_async_copy(x_hbm, xv, local_sem.at[1]),
        "b": pltpu.make_async_copy(bu_hbm, agb.at[z], local_sem.at[2]),
        "a": pltpu.make_async_copy(ad_hbm, aga.at[z], local_sem.at[3]),
        "w": pltpu.make_async_copy(w_hbm, wv, local_sem.at[4]),
        "table": pltpu.make_async_copy(table_hbm, table_ref, local_sem.at[5]),
        "gai": pltpu.make_async_copy(gai_hbm, gai_ref, local_sem.at[6]),
        "len": pltpu.make_async_copy(len_hbm, len_ref, local_sem.at[7]),
    }

    def plane_copy(unit, i, src, dst):
        xx, cc = column(PEERS[i])
        return pltpu.make_async_remote_copy(
            src_ref=src, dst_ref=dst, send_sem=x_send.at[unit, i], recv_sem=x_recv.at[unit, i],
            device_id=(at(xx, z, cc), y), device_id_type=MESH,
        )

    def token_copy(unit, i):
        kind, first, count = TOKENS[unit]
        packed, landed = ((gp, tokg), (xp, tokx))[kind]
        xx, cc = column(PEERS[i])
        entries = pl.ds(first, count)
        return plane_copy(unit, i, packed.at[xx * NC + cc, entries], landed.at[entries, p])

    def meta_copy(i):
        xx, cc = column(PEERS[i])
        return plane_copy(len(TOKENS) + 1, i, meta_s.at[xx * NC + cc], meta_r.at[p])

    def lora_copy(i):
        xx, cc = column(PEERS[i])
        return plane_copy(len(TOKENS), i, lora_s.at[:, xx * NC + cc], lora_r.at[p])

    def ag_copy(u, d, h, f):
        own = (bu_hbm, ad_hbm)[u]
        buf = (agb, aga)[u]
        rows = pl.ds(f * HALF, HALF)
        source = zplus(-(h - 1) if d == 0 else h - 1)
        src = own.at[rows] if h == 1 else buf.at[source, rows]
        return pltpu.make_async_remote_copy(
            src_ref=src, dst_ref=buf.at[source, rows],
            send_sem=ag_send.at[u, d, h - 1, f], recv_sem=ag_recv.at[u, d, h - 1, f],
            device_id=(at(x, zplus(DIRS[d]), c), y), device_id_type=MESH,
        )

    def rs_copy(u, d, h, f):
        return pltpu.make_async_remote_copy(
            src_ref=rs_s.at[u, d, h - 1, f], dst_ref=rs_r.at[u, d, h - 1, f],
            send_sem=rs_send.at[u, d, h - 1, f], recv_sem=rs_recv.at[u, d, h - 1, f],
            device_id=(at(x, zplus(DIRS[d]), c), y), device_id_type=MESH,
        )

    def low_copy(u, part, dy):
        return pltpu.make_async_remote_copy(
            src_ref=low_s.at[u, part], dst_ref=low_r.at[u, part, dy - 1],
            send_sem=low_send.at[u, part, dy - 1], recv_sem=low_recv.at[u, part, dy - 1],
            device_id=(me, lax.rem(y + dy, NY)), device_id_type=MESH,
        )

    def base_copy(dy, f):
        hop = dy if dy != 2 else (1, NY - 1)[f]
        rows = pl.ds(f * (toks // PIECES), toks // PIECES)
        return pltpu.make_async_remote_copy(
            src_ref=base_s.at[dy, rows], dst_ref=base_r.at[dy - 1, rows],
            send_sem=base_send.at[dy - 1, f], recv_sem=base_recv.at[dy - 1, f],
            device_id=(me, lax.rem(y + hop, NY)), device_id_type=MESH,
        )

    def halves(h):
        return FIRST + SECOND if h < HOPS else FIRST

    barrier = pltpu.get_barrier_semaphore()
    partners = [(at(*_xzc(column(k), z)), y) for k in PEERS]
    partners += [(at(x, zplus(d), c), y) for d in DIRS]
    partners += [(me, lax.rem(y + dy, NY)) for dy in range(1, NY)]
    for partner in partners:
        pl.semaphore_signal(barrier, inc=1, device_id=partner, device_id_type=MESH)
    small = ("table", "gai", "len")
    for name in small + ("g", "x", "w", "b", "a"):
        locals_[name].start()
    for name in small:
        locals_[name].wait()

    ng = gai_ref.shape[1]
    eye = iota((ng, ng), 0) == iota((ng, ng), 1)

    def to_col(row):
        return jnp.sum(jnp.where(eye, row, 0.0), axis=1, keepdims=True)

    def to_row(col):
        return jnp.sum(jnp.where(eye, col, 0.0), axis=0, keepdims=True)

    gai_col = to_col(gai_ref[...].astype(F32)).astype(jnp.int32)
    len_row = len_ref[...].astype(F32)
    len_col = to_col(len_row)
    n_adapters = table_ref.shape[1]
    slot = jnp.sum(
        jnp.where(iota((ng, n_adapters), 1) == gai_col, table_ref[...].astype(F32), 0.0), axis=1, keepdims=True
    ).astype(jnp.int32)
    local = slot & (SLOTS - 1)
    owner_c = (slot >> 3) & 1
    owner_z = (slot >> 4) & (NZ - 1)
    owner_x = slot >> 7
    ahead = (owner_z + (NZ - z)) & (NZ - 1)
    entry = jnp.maximum(NZ - 1 - 2 * jnp.minimum(ahead, NZ - ahead) + jnp.where(ahead > HOPS, 1, 0), 0)
    pair = (owner_x * NC + owner_c) * NZ + entry
    start = jnp.sum(jnp.where(iota((ng, ng), 1) < iota((ng, ng), 0), len_row, 0.0), axis=1, keepdims=True)
    shift = (pair * CAP).astype(F32) - start
    end = start + len_col
    t_row = iota((ng, toks), 1).astype(F32)
    idx_row[...] = jnp.sum(
        jnp.where((t_row >= start) & (t_row < end), shift + t_row, 0.0), axis=0, keepdims=True
    ).astype(jnp.int32)
    t_col = iota((toks, ng), 0).astype(F32)
    idx_col[...] = jnp.sum(
        jnp.where((t_col >= to_row(start)) & (t_col < to_row(end)), to_row(shift) + t_col, 0.0), axis=1, keepdims=True
    ).astype(jnp.int32)
    pairs = PLANE * NZ
    slot_of_pair = jnp.sum(
        jnp.where(iota((pairs, ng), 0) == to_row(pair.astype(F32)).astype(jnp.int32), to_row(local.astype(F32)) + 1.0, 0.0),
        axis=1, keepdims=True,
    ).astype(jnp.int32)
    mask = jnp.where((iota((pairs, ROWS), 1) >> 4) + 1 == slot_of_pair, 1.0, 0.0)
    meta_s[...] = mask.reshape(PLANE, NZ, ROWS)
    meta_r[pl.ds(p, 1)] = meta_s[pl.ds(p, 1)]

    pl.semaphore_wait(barrier, len(partners))

    for d, f in halves(1):
        ag_copy(0, d, 1, f).start()

    for i in range(len(PEERS)):
        meta_copy(i).start()

    def pack(source, packed, q):
        hot = jnp.where(iota((ROWS, toks), 0) + q * ROWS == idx_row[...], 1.0, 0.0).astype(BF16)
        packed[q] = mm(hot, source[...]).astype(BF16).reshape(NZ, CAP, -1)

    def forward(u, h, part):
        for d, f in part:
            source = zplus(-h if d == 0 else h)
            buf = (agb, aga)[u]
            landed = buf.at[source, pl.ds(f * HALF, HALF)]
            pltpu.make_async_remote_copy(
                src_ref=landed, dst_ref=landed, send_sem=ag_send.at[u, d, h - 1, f],
                recv_sem=ag_recv.at[u, d, h - 1, f], device_id=(at(x, zplus(DIRS[d]), c), y), device_id_type=MESH,
            ).wait_recv()
            if h < HOPS and (d, f) in halves(h + 1):
                ag_copy(u, d, h + 1, f).start()

    def base_block(dy):
        block = lax.rem(y + dy, NY)
        width = 256

        def tile(n, carry):
            rows = pl.ds(pl.multiple_of(block * wv.shape[1] + n * width, width), width)
            cols = pl.ds(pl.multiple_of(n * width, width), width)
            base_s[dy, :, cols] = mm(gv[...], wv[rows, :], NT).astype(BF16)
            return carry

        lax.fori_loop(0, wv.shape[1] // width, tile, 0)

    def base_relay(dy, f):
        base_copy(2, f).wait_recv()
        rows = pl.ds(f * (toks // PIECES), toks // PIECES)
        base_s[dy, rows, :] = (base_s[dy, rows, :].astype(F32) + base_r[1, rows, :].astype(F32)).astype(BF16)
        base_copy(dy, f).start()

    def select(e, transposed):
        a, b = iota((ROWS, ROWS), 0), iota((ROWS, ROWS), 1)
        narrow, broad = (a, b) if transposed else (b, a)
        return jnp.where(narrow == e * RANK + (broad & (RANK - 1)), 1.0, 0.0).astype(BF16)

    toks_of = (tokx, tokg)
    project_of = (tokg, tokx)
    maps_of = (agb, aga)

    def project(u, part):
        first, count = LOWS[u][part]

        def block(e, carry):
            wide_p = mm(project_of[u][e].reshape(ROWS, -1), maps_of[u][owner_z_of(e)], NT) * masks[e]
            part_low = mm(wide_p.astype(BF16), select(e, False))
            low_acc[...] = jnp.where(e == first, part_low, low_acc[...] + part_low)
            return carry

        lax.fori_loop(first, first + count, block, 0)
        low_s[u, part] = low_acc[...].astype(BF16)
        for dy in (2, 1, 3):
            low_copy(u, part, dy).start()

    def spread(u, part):
        total = low_s[u, part].astype(F32)
        for dy in range(1, NY):
            low_copy(u, part, dy).wait_recv()
            total = total + low_r[u, part, dy - 1].astype(F32)
        low = total.astype(BF16)
        first, count = LOWS[u][part]

        def block(e, carry):
            twice = mm(low, select(e, True)) * (2.0 * masks[e])
            if u == 0:
                wide[e] = twice.astype(BF16)
            wide_t[u, e] = twice.T.astype(BF16)
            return carry

        lax.fori_loop(first, first + count, block, 0)

    def lora(distance):
        e = entry_of(distance)
        lora_s[e] = mm(wide[e], aga[zplus(distance)]).astype(BF16).reshape(PLANE, CAP, -1)

    def term(u, distance, f):
        e = entry_of(distance)
        return mm(wide_t[u, e, f * HALF : (f + 1) * HALF, :], toks_of[u][e].reshape(ROWS, -1))

    def rs_target(d, h):
        return (HOPS + 1 - h) if d == 0 else -(HOPS + 1 - h)

    def rs_init(u):
        for h, part in ((1, FIRST), (2, SECOND)):
            for d, f in part:
                rs_s[u, d, h - 1, f] = term(u, rs_target(d, h), f).astype(BF16)
                rs_copy(u, d, h, f).start()

    def rs_step(u, h, part):
        for d, f in part:
            rs_copy(u, d, h, f).wait_recv()
            total = rs_r[u, d, h - 1, f].astype(F32) + term(u, rs_target(d, h + 1), f)
            rs_s[u, d, h, f] = total.astype(BF16)
            rs_copy(u, d, h + 1, f).start()

    def rs_last(u):
        out = (dgrad_ref, ugrad_ref)[u]
        own = [term(u, 0, f) for f in (0, 1)]
        for d, f in SECOND:
            rs_copy(u, d, HOPS, f).wait_recv()
            own[f] = own[f] + rs_r[u, d, HOPS - 1, f].astype(F32)
        for d, f in FIRST:
            rs_copy(u, d, HOPS, f).wait_recv()
            out[f * HALF : (f + 1) * HALF, :] = own[f] + rs_r[u, d, HOPS - 1, f].astype(F32)

    def finish(n, carry):
        rows = pl.ds(pl.multiple_of(n * ROWS, ROWS), ROWS)
        hot = jnp.where(iota((ROWS, PLANE * ROWS), 1) == idx_col[rows, :], 1.0, 0.0).astype(BF16)
        total = mm(hot, lora_r[...].reshape(PLANE * ROWS, -1)) + base_s[0, rows, :].astype(F32)
        for dy in (1, NY - 1):
            total = total + base_r[dy - 1, rows, :].astype(F32)
        dx_ref[rows, :] = total.astype(BF16)
        return carry

    def own_tokens(packed, landed):
        pack(gv if packed is gp else xv, packed, p)
        landed[:, pl.ds(p, 1)] = packed[pl.ds(p, 1)].reshape(NZ, 1, CAP, -1)

    every = range(len(PEERS))

    def ring_sent(u, hops):
        for h in hops:
            for d, f in FIRST + SECOND if h > 1 else FIRST:
                rs_copy(u, d, h, f).wait_send()

    def plane_sent():
        for i in every:
            meta_copy(i).wait_send()
            for unit in range(len(TOKENS)):
                token_copy(unit, i).wait_send()

    def gather_sent(u):
        for h in range(1, HOPS + 1):
            for d, f in halves(h):
                ag_copy(u, d, h, f).wait_send()

    def tensor_sent():
        for dy in range(1, NY):
            for u in (0, 1):
                for part in range(len(LOWS[u])):
                    low_copy(u, part, dy).wait_send()
            for f in range(PIECES):
                base_copy(dy, f).wait_send()

    locals_["g"].wait()
    for i in every:
        xx, cc = column(PEERS[i])
        pack(gv, gp, xx * NC + cc)
        token_copy(0, i).start()
    forward(0, 1, FIRST)
    locals_["w"].wait()
    base_block(2)
    for f in (0, 1):
        base_copy(2, f).start()
    forward(0, 1, SECOND)
    base_block(1)
    base_copy(1, 1).start()
    forward(0, 2, FIRST)
    locals_["x"].wait()
    for i in every[:4]:
        xx, cc = column(PEERS[i])
        pack(xv, xp, xx * NC + cc)
        token_copy(1, i).start()
    forward(0, 2, SECOND)
    base_block(3)
    base_copy(3, 0).start()
    for i in every[4:]:
        xx, cc = column(PEERS[i])
        pack(xv, xp, xx * NC + cc)
        token_copy(1, i).start()
    for unit in range(2, len(TOKENS)):
        for i in every:
            token_copy(unit, i).start()
    forward(0, 3, FIRST)
    for d, f in FIRST:
        ag_copy(1, d, 1, f).start()
    own_tokens(gp, tokg)
    for i in every:
        meta_copy(i).wait_recv()
    for e in range(NZ):
        masks[e] = jnp.broadcast_to(meta_r[:, e : e + 1, :], (PLANE, CAP, ROWS)).reshape(ROWS, ROWS)
    forward(0, 3, SECOND)
    for d, f in SECOND:
        ag_copy(1, d, 1, f).start()
    own_tokens(xp, tokx)
    forward(0, HOPS, FIRST)
    locals_["b"].wait()

    def landed(unit):
        for i in every:
            token_copy(unit, i).wait_recv()

    landed(0)
    project(0, 0)
    forward(1, 1, FIRST)
    forward(1, 1, SECOND)
    base_block(0)
    forward(1, 2, FIRST)
    landed(2)
    project(0, 1)
    base_relay(1, 0)
    base_relay(3, 1)
    locals_["a"].wait()
    forward(1, 2, SECOND)
    forward(1, 3, FIRST)
    forward(1, 3, SECOND)
    spread(0, 0)
    landed(1)
    rs_init(0)
    lora(3)
    lora(-3)
    forward(1, HOPS, FIRST)
    lora(HOPS)
    spread(0, 1)
    lora(2)
    lora(-2)
    rs_step(0, 1, FIRST)
    landed(3)
    project(1, 0)
    landed(4)
    project(0, 2)
    rs_step(0, 2, SECOND)
    rs_step(0, 2, FIRST)
    spread(0, 2)
    for distance in (0, 1, -1):
        lora(distance)
    for i in every:
        lora_copy(i).start()
    lora_r[pl.ds(p, 1)] = lora_s[:, pl.ds(p, 1)].reshape(1, NZ, CAP, -1)
    landed(5)
    rs_step(0, 3, SECOND)
    landed(6)
    project(1, 1)
    rs_step(0, 3, FIRST)
    spread(1, 0)
    rs_init(1)
    rs_last(0)
    gather_sent(0)
    gather_sent(1)
    rs_step(1, 1, FIRST)
    plane_sent()
    rs_step(1, 2, SECOND)
    spread(1, 1)
    ring_sent(0, range(1, HOPS + 1))
    rs_step(1, 2, FIRST)
    tensor_sent()
    rs_step(1, 3, SECOND)
    rs_step(1, 3, FIRST)
    for i in every:
        lora_copy(i).wait_recv()
    for f in range(PIECES):
        for dy in (1, NY - 1):
            base_copy(dy, f).wait_recv()
    lax.fori_loop(0, toks // ROWS, finish, 0)
    for i in every:
        lora_copy(i).wait_send()
    ring_sent(1, range(1, HOPS))
    rs_last(1)

    ring_sent(1, (HOPS,))


def _xzc(xc, z):
    return xc[0], z, xc[1]


def emit(*refs):
    copies = [pltpu.make_async_copy(refs[i], refs[3 + i], refs[6].at[i]) for i in range(3)]
    for copy in copies:
        copy.start()
    for copy in copies:
        copy.wait()


def on_device(
    activations,
    output_gradient,
    frozen_weight,
    adapter_down_weight,
    adapter_up_weight,
    adapter_slot_table,
    group_adapter_index,
    group_token_length,
):
    toks, feats = activations.shape
    own = adapter_down_weight.shape[0]
    any_spec = pl.BlockSpec(memory_space=pl.ANY)
    vmem_spec = pl.BlockSpec(memory_space=pltpu.VMEM)
    dma = pltpu.SemaphoreType.DMA
    n = len(PEERS)
    results = pl.pallas_call(
        kernel,
        out_shape=(
            pltpu.VMEM((toks, feats), BF16),
            pltpu.VMEM((own, feats), F32),
            pltpu.VMEM((own, feats), F32),
        ),
        in_specs=[any_spec] * 8,
        out_specs=(vmem_spec,) * 3,
        scratch_shapes=[
            pltpu.VMEM((toks, feats), BF16),
            pltpu.VMEM((toks, feats), BF16),
            pltpu.VMEM(frozen_weight.shape, BF16),
            pltpu.VMEM((PLANE, NZ, CAP, feats), BF16),
            pltpu.VMEM((PLANE, NZ, CAP, feats), BF16),
            pltpu.VMEM((NZ, PLANE, CAP, feats), BF16),
            pltpu.VMEM((NZ, PLANE, CAP, feats), BF16),
            pltpu.VMEM((NZ, ROWS, feats), BF16),
            pltpu.VMEM((NZ, ROWS, feats), BF16),
            pltpu.VMEM((PLANE, NZ, ROWS), F32),
            pltpu.VMEM((PLANE, NZ, ROWS), F32),
            pltpu.VMEM((NZ, ROWS, ROWS), F32),
            pltpu.VMEM((ROWS, ROWS), F32),
            pltpu.VMEM((2, 3, ROWS, ROWS), BF16),
            pltpu.VMEM((2, 3, NY - 1, ROWS, ROWS), BF16),
            pltpu.VMEM((NZ, ROWS, ROWS), BF16),
            pltpu.VMEM((2, NZ, ROWS, ROWS), BF16),
            pltpu.VMEM((NY, toks, feats), BF16),
            pltpu.VMEM((NY - 1, toks, feats), BF16),
            pltpu.VMEM((NZ, PLANE, CAP, feats), BF16),
            pltpu.VMEM((PLANE, NZ, CAP, feats), BF16),
            pltpu.VMEM((2, 2, HOPS, 2, HALF, feats), BF16),
            pltpu.VMEM((2, 2, HOPS, 2, HALF, feats), BF16),
            pltpu.VMEM((1, toks), jnp.int32),
            pltpu.VMEM((toks, 1), jnp.int32),
            pltpu.VMEM((1, adapter_slot_table.shape[0]), jnp.int32),
            pltpu.VMEM(group_adapter_index.shape, jnp.int32),
            pltpu.VMEM(group_token_length.shape, jnp.int32),
            dma((8,)),
            dma((len(TOKENS) + 2, n)),
            dma((len(TOKENS) + 2, n)),
            dma((2, 2, HOPS, 2)),
            dma((2, 2, HOPS, 2)),
            dma((2, 2, HOPS, 2)),
            dma((2, 2, HOPS, 2)),
            dma((2, 3, NY - 1)),
            dma((2, 3, NY - 1)),
            dma((NY - 1, PIECES)),
            dma((NY - 1, PIECES)),
        ],
        compiler_params=pltpu.CompilerParams(
            collective_id=0, has_side_effects=True, vmem_limit_bytes=60 * 1024 * 1024
        ),
        name="lora_backward",
    )(
        activations,
        output_gradient,
        frozen_weight,
        adapter_down_weight,
        adapter_up_weight,
        adapter_slot_table.reshape(1, -1),
        group_adapter_index,
        group_token_length,
    )
    return pl.pallas_call(
        emit,
        out_shape=tuple(jax.ShapeDtypeStruct(r.shape, r.dtype) for r in results),
        in_specs=[vmem_spec] * 3,
        out_specs=(any_spec,) * 3,
        scratch_shapes=[dma((3,))],
        name="emit",
    )(*(pltpu.with_memory_space_constraint(r, pltpu.VMEM) for r in results))


def solution(mesh):
    in_specs = (
        P("adapter", "tensor"),
        P("adapter", "tensor"),
        P(None, "tensor"),
        P("adapter", "tensor"),
        P("adapter", "tensor"),
        P(),
        P("adapter", None),
        P("adapter", None),
    )
    out_specs = (P("adapter", "tensor"), P("adapter", "tensor"), P("adapter", "tensor"))
    return jax.shard_map(
        on_device, mesh=mesh, in_specs=in_specs, out_specs=out_specs, check_vma=False
    )
```
